256 devices in a mesh: group: 4 (over y), inner: 64 (over x, z, core).
Axes of the slice: x: 4, y: 4, z: 8, core: 2. Of those that a mesh axis runs over, the one named last changes fastest.
Arguments:
- tokens: bfloat16 [8192, 2048], P(('group', 'inner')), may hold values from -6 to 6
- upstream: bfloat16 [8192, 2048], P(('group', 'inner')), may hold values from -6 to 6
- gate_weights: float32 [8192, 8], P(('group', 'inner')), may hold values from 0.05 to 0.5
- group_choice: int32 [8192, 4], P(('group', 'inner')), may hold values from 0 to 7, all different within a row
- pair_pick: int32 [8192, 4, 2], P(('group', 'inner')), may hold values from 0 to 15, all different within a row
- w_gate: bfloat16 [256, 1, 2048, 384], P(('group', 'inner')), may hold values from -0.125 to 0.125
- w_up: bfloat16 [256, 1, 2048, 384], P(('group', 'inner')), may hold values from -0.125 to 0.125
- w_down: bfloat16 [256, 1, 384, 2048], P(('group', 'inner')), may hold values from -0.21875 to 0.21875
Outputs:
- mixed: bfloat16 [8192, 2048], P(('group', 'inner'))
- grad_tokens: bfloat16 [8192, 2048], P(('group', 'inner'))
- grad_gate: bfloat16 [256, 1, 2048, 384], P(('group', 'inner'))
- grad_up: bfloat16 [256, 1, 2048, 384], P(('group', 'inner'))
- grad_down: bfloat16 [256, 1, 384, 2048], P(('group', 'inner'))
The draws below stay inside these ranges and needn't reach their ends.
Inputs may be any that keep to these rules, and one draw needn't show every extreme that they name: `group_choice`: each token names 4 different routing groups. `pair_pick`: the picks of one token within one routing group differ.
All inputs are finite; a program needn't handle non-finite values.
Results may differ from the reference program's by a relative error of at most 0.015.
Values may be sent and summed in bfloat16 or wider, within the bound.
A program may use at most 128 MiB of HBM per device.

```python
import jax
import jax.numpy as jnp
from jax import lax

D = 2048
FF = 768
EXPERTS = 128
TOPK = 8
RGROUPS = 8
GLIMIT = 4
TOK_DEV = 32
CAP = 2
EXP_DEV = 1
SPLIT = 2
FL = 384
TOKENS = 8192
N_GROUP = 4
N_INNER = 64


def level_of(rng, extent, pieces, smallest, high):
    factor_of = 1.0
    for position, parts in pieces:
        draws = jax.random.uniform(jax.random.fold_in(jax.random.fold_in(rng, 6), position), (parts,), jnp.float32, smallest / len(pieces), high / len(pieces))
        factor_of = factor_of * jnp.repeat(jnp.exp(draws), extent[position] // parts).reshape((-1,) + (1,) * (len(extent) - 1 - position))
    return factor_of


def picks_of(own_key, rows, count, top, lift):
    sequence = jax.random.permutation(jax.random.fold_in(own_key, 1), count)
    pull = sequence
    for power in range(3):
        pull = pull * pull // count
    pull = pull * lift // count
    tickets = jax.random.randint(jax.random.fold_in(own_key, 2), (rows, count), 0, 4096) + pull
    sure = jax.random.permutation(jax.random.fold_in(own_key, 3), rows)[jnp.arange(count) % rows]
    tickets = jnp.where(jnp.arange(rows)[:, None] == sure[None, :], 1 << 14, tickets)
    score = tickets * count + jnp.arange(count)
    return lax.top_k(score.astype(jnp.int32), top)[1].astype(jnp.int32)


def normal_values(own_key, shape, width, most, cuts=(), held_as=jnp.bfloat16):
    result = width * jax.random.normal(own_key, shape, jnp.float32)
    if cuts:
        result = result * level_of(own_key, shape, cuts, -0.22, 0.18)
    return jnp.clip(result, -most, most).astype(held_as)


def setup_inputs(seed: int = 0) -> dict:
    splits = jax.random.split(jax.random.key(seed), 9)
    return {
        "tokens": normal_values(splits[0], (TOKENS, D), 1.0, 6.0, ((0, 256),)),
        "upstream": normal_values(splits[1], (TOKENS, D), 1.0, 6.0, ((0, 256),)),
        "gate_weights": jnp.clip(0.05 + 0.45 * jax.random.uniform(splits[2], (TOKENS, TOPK), jnp.float32) ** level_of(splits[2], (TOKENS, TOPK), ((0, 256),), -0.2, 0.2), 0.05, 0.5),
        "group_choice": picks_of(splits[3], TOKENS, RGROUPS, GLIMIT, 4096),
        "pair_pick": picks_of(splits[4], TOKENS * GLIMIT, EXPERTS // RGROUPS, TOPK // GLIMIT, 1024).reshape((TOKENS, GLIMIT, TOPK // GLIMIT)),
        "w_gate": normal_values(splits[5], (N_GROUP * N_INNER, EXP_DEV, D, FL), D ** -0.5, 0.125, ((0, 256),)),
        "w_up": normal_values(splits[6], (N_GROUP * N_INNER, EXP_DEV, D, FL), D ** -0.5, 0.125, ((0, 256),)),
        "w_down": normal_values(splits[7], (N_GROUP * N_INNER, EXP_DEV, FL, D), FF ** -0.5, 0.21875, ((0, 256),)),
    }


def expert_ids(group_choice, pair_pick):
    per_group = EXPERTS // RGROUPS
    joined = group_choice[:, :, None] * per_group + pair_pick
    return joined.reshape(joined.shape[0], TOPK).astype(jnp.int32)


def slot_table(ids, weights):
    flat = ids.reshape(-1)
    number = flat.shape[0]
    onehot = (flat[:, None] == jnp.arange(EXPERTS, dtype=jnp.int32)[None, :]).astype(jnp.int32)
    before = jnp.cumsum(onehot, axis=0) - onehot
    rank = jnp.sum(before * onehot, axis=1)
    target = jnp.where(rank < CAP, flat * CAP + rank, EXPERTS * CAP).astype(jnp.int32)
    owner = (jnp.arange(number, dtype=jnp.int32) // TOPK).astype(jnp.int32)
    empty = ids.shape[0]
    slot_token = jnp.full((EXPERTS * CAP + 1,), empty, jnp.int32).at[target].set(owner)[:-1]
    slot_weight = jnp.zeros((EXPERTS * CAP + 1,), jnp.float32).at[target].set(weights.reshape(-1))[:-1]
    return slot_token, slot_weight


def reference(tokens, upstream, gate_weights, group_choice, pair_pick, w_gate, w_up, w_down):
    blocks = tokens.shape[0] // TOK_DEV
    ids = expert_ids(group_choice, pair_pick).reshape(blocks, TOK_DEV, TOPK)
    slot_token, slot_weight = jax.vmap(slot_table)(ids, gate_weights.reshape(blocks, TOK_DEV, TOPK))
    offset = (jnp.arange(blocks, dtype=jnp.int32) * (TOK_DEV + 1))[:, None]
    rows = (slot_token + offset).astype(jnp.int32).reshape(blocks, EXPERTS, CAP).transpose(1, 0, 2).reshape(EXPERTS, blocks * CAP)
    scales = slot_weight.reshape(blocks, EXPERTS, CAP).transpose(1, 0, 2).reshape(EXPERTS, blocks * CAP)
    filler = jnp.zeros((blocks, 1, D), tokens.dtype)
    x_pad = jnp.concatenate([tokens.reshape(blocks, TOK_DEV, D), filler], axis=1).reshape(-1, D)
    dy_pad = jnp.concatenate([upstream.reshape(blocks, TOK_DEV, D), filler], axis=1).reshape(-1, D)
    owners = EXPERTS // EXP_DEV
    gate_all = w_gate.reshape(owners, SPLIT, EXP_DEV, D, FL)
    up_all = w_up.reshape(owners, SPLIT, EXP_DEV, D, FL)
    down_all = w_down.reshape(owners, SPLIT, EXP_DEV, FL, D)

    def step(carry, expert):
        y_acc, dx_acc = carry
        owner = expert // EXP_DEV
        within = expert % EXP_DEV
        w_g = gate_all[owner, :, within].transpose(1, 0, 2).reshape(D, FF)
        w_u = up_all[owner, :, within].transpose(1, 0, 2).reshape(D, FF)
        w_d = down_all[owner, :, within].reshape(FF, D)
        index = rows[expert]
        scale = scales[expert]
        x_rows = x_pad[index]
        dout = (scale[:, None] * dy_pad[index].astype(jnp.float32)).astype(jnp.bfloat16)
        gate = jnp.dot(x_rows, w_g, preferred_element_type=jnp.float32)
        upv = jnp.dot(x_rows, w_u, preferred_element_type=jnp.float32)
        sig = jax.nn.sigmoid(gate)
        act = gate * sig
        hidden = (act * upv).astype(jnp.bfloat16)
        out_rows = jnp.dot(hidden, w_d, preferred_element_type=jnp.float32).astype(jnp.bfloat16)
        dh = jnp.dot(dout, w_d.T, preferred_element_type=jnp.float32)
        dgate = (dh * upv * sig * (1.0 + gate * (1.0 - sig))).astype(jnp.bfloat16)
        dup = (dh * act).astype(jnp.bfloat16)
        dx_rows = (jnp.dot(dgate, w_g.T, preferred_element_type=jnp.float32)
                   + jnp.dot(dup, w_u.T, preferred_element_type=jnp.float32)).astype(jnp.bfloat16)
        g_gate = jnp.dot(x_rows.T, dgate, preferred_element_type=jnp.float32).astype(jnp.bfloat16)
        g_up = jnp.dot(x_rows.T, dup, preferred_element_type=jnp.float32).astype(jnp.bfloat16)
        g_down = jnp.dot(hidden.T, dout, preferred_element_type=jnp.float32).astype(jnp.bfloat16)
        y_acc = y_acc.at[index].add(scale[:, None] * out_rows.astype(jnp.float32))
        dx_acc = dx_acc.at[index].add(dx_rows.astype(jnp.float32))
        return (y_acc, dx_acc), (g_gate, g_up, g_down)

    start = (jnp.zeros((x_pad.shape[0], D), jnp.float32), jnp.zeros((x_pad.shape[0], D), jnp.float32))
    (y_acc, dx_acc), (g_gate, g_up, g_down) = lax.scan(step, start, jnp.arange(EXPERTS, dtype=jnp.int32))
    mixed = y_acc.reshape(blocks, TOK_DEV + 1, D)[:, :TOK_DEV].reshape(-1, D).astype(jnp.bfloat16)
    grad_tokens = dx_acc.reshape(blocks, TOK_DEV + 1, D)[:, :TOK_DEV].reshape(-1, D).astype(jnp.bfloat16)
    grad_gate = g_gate.reshape(owners, EXP_DEV, D, SPLIT, FL).transpose(0, 3, 1, 2, 4).reshape(owners * SPLIT, EXP_DEV, D, FL)
    grad_up = g_up.reshape(owners, EXP_DEV, D, SPLIT, FL).transpose(0, 3, 1, 2, 4).reshape(owners * SPLIT, EXP_DEV, D, FL)
    grad_down = g_down.reshape(owners, EXP_DEV, SPLIT, FL, D).transpose(0, 2, 1, 3, 4).reshape(owners * SPLIT, EXP_DEV, FL, D)
    return (mixed, grad_tokens, grad_gate, grad_up, grad_down)
```

```python
import functools

import jax
import jax.numpy as jnp
from jax import lax
from jax.experimental import pallas as pl
from jax.experimental.pallas import tpu as pltpu
from jax.sharding import PartitionSpec as P

MESH = pl.DeviceIdType.MESH
F32 = jnp.float32
BF16 = jnp.bfloat16

XDIM = 4
CHUNKS = 2

NT_DIMS = (((1,), (1,)), ((), ()))
TN_DIMS = (((0,), (0,)), ((), ()))


def dot(a, b, dims=(((1,), (0,)), ((), ()))):
    return lax.dot_general(a, b, dims, preferred_element_type=F32)


def kernel(
    cfg,
    tok_ref, dy_ref, gw_ref, gc_ref, pp_ref, wg_hbm, wu_hbm, wd_hbm,
    mixed_ref, gt_ref, gg_hbm, gu_hbm, gd_hbm,
    zx, zg, xs, xr, amat, comb, wcol, wgu, wd, acc, dh, hid, dgu,
    osend, orecv, rsend, rrecv, part, tsend, trecv, ggu, ggd,
    w_sem, g_sem, ags_sem, agr_sem, zgs_sem, zgr_sem, xs_sem, xr_sem, fs_sem, fr_sem,
    os_sem, or_sem, rs_sem, rr_sem, ts_sem, tr_sem,
):
    NX, NY, NZ, NC, E = cfg
    NQ = NX * NY
    T, D = tok_ref.shape
    CW = D // NC
    FL = wd.shape[0]
    NB = NZ
    S2 = 2 * NB
    R = NQ * S2
    NT = NB * T
    HP, HM = NZ // 2, NZ - 1 - NZ // 2
    per_group = E // (gc_ref.shape[1] * 2)

    y = lax.axis_index("group")
    inner = lax.axis_index("inner")
    core = lax.rem(inner, 2)
    z = lax.rem(lax.div(inner, 2), NZ)
    x = lax.div(inner, 2 * NZ)
    q_me = y * NX + x

    def place(px, pz, pc):
        return (px * NZ + pz) * 2 + pc

    z_up = (y, place(x, lax.rem(z + 1, NZ), core))
    z_down = (y, place(x, lax.rem(z + NZ - 1, NZ), core))
    sibling = (y, place(x, z, 1 - core))

    def plane(k):
        ty = lax.rem(y + lax.div(k, NX), NY)
        tx = lax.rem(x + lax.rem(k, NX), NX)
        return ty * NX + tx, (ty, place(tx, z, core))

    def rcopy(src, dst, ssem, rsem, dev):
        return pltpu.make_async_remote_copy(
            src_ref=src, dst_ref=dst, send_sem=ssem, recv_sem=rsem, device_id=dev, device_id_type=MESH
        )

    barrier = pltpu.get_barrier_semaphore()
    for dev in (z_up, z_down, sibling):
        pl.semaphore_signal(barrier, inc=1, device_id=dev, device_id_type=MESH)

    def greet(k, carry):
        _, dev = plane(k)
        pl.semaphore_signal(barrier, inc=1, device_id=dev, device_id_type=MESH)
        return carry

    lax.fori_loop(1, NQ, greet, 0)

    loads = [
        pltpu.make_async_copy(wg_hbm, wgu.at[:, pl.ds(0, FL)], w_sem.at[0]),
        pltpu.make_async_copy(wu_hbm, wgu.at[:, pl.ds(FL, FL)], w_sem.at[1]),
        pltpu.make_async_copy(wd_hbm, wd, w_sem.at[2]),
    ]
    for c in loads:
        c.start()

    lane = lax.broadcasted_iota(jnp.int32, (T, E), 1)
    table = jnp.zeros((T, E), F32)
    for k in range(gw_ref.shape[1]):
        ids = gc_ref[:, k // 2 : k // 2 + 1] * per_group + pp_ref[:, k : k + 1]
        table = table + jnp.where(ids == lane, gw_ref[:, k : k + 1], 0.0)
    hi = table.astype(BF16)
    zg[0, :, 0:E] = hi
    zg[0, :, E : 2 * E] = (table - hi.astype(F32)).astype(BF16)
    for c in range(NC):
        zx[c, 0] = tok_ref[:, c * CW : (c + 1) * CW]
        zx[NC + c, 0] = dy_ref[:, c * CW : (c + 1) * CW]

    pl.semaphore_wait(barrier, NQ + 2)

    def ring(buf, ssem, rsem, h):
        out = [rcopy(buf.at[h - 1], buf.at[h], ssem, rsem.at[h - 1], z_up)]
        if h <= HM:
            src = buf.at[0] if h == 1 else buf.at[HP + h - 1]
            out.append(rcopy(src, buf.at[HP + h], ssem, rsem.at[HP + h - 1], z_down))
        return out

    def ag(c, h):
        if c < 0:
            return ring(zg, zgs_sem.at[0], zgr_sem, h)
        return ring(zx.at[c], ags_sem.at[c], agr_sem.at[c], h)

    def ag_send(c, h):
        for d in ag(c, h):
            d.start()

    def ag_wait(c, h):
        for d in ag(c, h):
            d.wait_recv()

    def xy_start(src, dst, ssem, rsem):
        own = pltpu.make_async_copy(src.at[q_me], dst.at[q_me], rsem)
        own.start()

        def body(k, carry):
            tq, dev = plane(k)
            rcopy(src.at[tq], dst.at[q_me], ssem, rsem, dev).start()
            return carry

        lax.fori_loop(1, NQ, body, 0)

    def xy_wait(src, dst, ssem, rsem):
        rcopy(src, dst, ssem, rsem, sibling).wait_recv()

    def gather(c):
        rows = dot(amat[...], zx[c].reshape(NT, CW))
        if c >= NC:
            rows = rows * wcol[:, 0:1]
        xs[c] = rows.astype(BF16).reshape(NQ, S2, CW)
        xy_start(xs.at[c], xr.at[c, 0], xs_sem.at[c], xr_sem.at[c])

    xs_list = list(range(NC))
    dy_list = list(range(NC, 2 * NC))
    ag_send(-1, 1)
    for c in xs_list:
        ag_send(c, 1)
    for h in range(2, HP + 1):
        for c in [-1] + xs_list:
            ag_wait(c, h - 1)
            ag_send(c, h)
    for c in dy_list:
        ag_send(c, 1)
    ag_wait(-1, HP)

    weights = zg[...].reshape(NT, 2 * E)
    whi = weights[:, 0:E].astype(F32)
    wlo = weights[:, E : 2 * E].astype(F32)
    routed = whi > 0.0
    tr_i = lax.broadcasted_iota(jnp.int32, (NT, NT), 0)
    tr_j = lax.broadcasted_iota(jnp.int32, (NT, NT), 1)
    lt = T.bit_length() - 1
    lower = jnp.where(((tr_i >> lt) == (tr_j >> lt)) & (tr_j < tr_i), 1.0, 0.0).astype(BF16)
    rank = dot(lower, jnp.where(routed, 1.0, 0.0).astype(BF16))
    first = jnp.where(routed & (rank < 0.5), 1.0, 0.0)
    second = jnp.where(routed & (rank > 0.5) & (rank < 1.5), 1.0, 0.0)
    picks = jnp.concatenate([first, second], axis=1)
    whi2 = picks * jnp.concatenate([whi, whi], axis=1)
    wlo2 = picks * jnp.concatenate([wlo, wlo], axis=1)
    picks = picks.astype(BF16)
    whi2 = whi2.astype(BF16)
    wlo2 = wlo2.astype(BF16)
    lz, ls, le = NZ.bit_length() - 1, S2.bit_length() - 1, E.bit_length() - 1

    def selector(shape, edim):
        e = lax.broadcasted_iota(jnp.int32, shape, edim)
        r = lax.broadcasted_iota(jnp.int32, shape, 1 - edim)
        ex = e & (E - 1)
        same = ((ex >> lz) == (r >> ls)) & ((ex & (NZ - 1)) == z) & ((e >> le) == (r & 1))
        return jnp.where(same, 1.0, 0.0).astype(BF16)

    def same_block(shape, tdim):
        t = lax.broadcasted_iota(jnp.int32, shape, tdim)
        r = lax.broadcasted_iota(jnp.int32, shape, 1 - tdim)
        return (t >> lt) == ((r >> 1) & (NB - 1))

    sel_t = selector((R, 2 * E), 1)
    mask_rt = same_block((R, NT), 1)
    amat[...] = jnp.where(mask_rt, dot(sel_t, picks, NT_DIMS), 0.0).astype(BF16)
    wsum = dot(sel_t, whi2, NT_DIMS) + dot(sel_t, wlo2, NT_DIMS)
    wcol[...] = jnp.broadcast_to(
        jnp.sum(jnp.where(mask_rt, wsum, 0.0), axis=1, keepdims=True), wcol.shape
    )

    for c in xs_list:
        ag_wait(c, HP)
        gather(c)

    sel = selector((2 * E, R), 0)
    mask_tr = same_block((NT, R), 0)
    for n, v in enumerate((picks, whi2, wlo2)):
        comb[n] = jnp.where(mask_tr, dot(v, sel), 0.0).astype(BF16)

    for h in range(2, HP + 1):
        for c in dy_list:
            ag_wait(c, h - 1)
            ag_send(c, h)
    for c in dy_list:
        ag_wait(c, HP)
        gather(c)

    def forward(c):
        xy_wait(xs.at[c], xr.at[c, 0], xs_sem.at[c], xr_sem.at[c])
        rcopy(xr.at[c, 0], xr.at[c, 1], fs_sem.at[c], fr_sem.at[c], sibling).start()

    def forward_wait(c):
        rcopy(xr.at[c, 0], xr.at[c, 1], fs_sem.at[c], fr_sem.at[c], sibling).wait_recv()

    def rows_of(c, half):
        return xr[c, half].reshape(R, CW)

    def gate_up(c, half):
        v = dot(rows_of(c, half), wgu[c * CW : (c + 1) * CW, :])
        acc[half] = v if c == 0 else acc[half] + v

    def hidden(half):
        v = acc[half]
        g, u = v[:, 0:FL], v[:, FL:]
        hid[half] = (g * jax.nn.sigmoid(g) * u).astype(BF16)

    def d_hidden(c, half):
        cols = slice((c - NC) * CW, (c - NC + 1) * CW)
        v = dot(rows_of(c, half), wd[:, cols], NT_DIMS)
        dh[half] = v if c == NC else dh[half] + v

    def d_gate_up(half):
        v = acc[half]
        g, u = v[:, 0:FL], v[:, FL:]
        s = jax.nn.sigmoid(g)
        d = dh[half]
        dgu[half, :, 0:FL] = (d * u * s * (1.0 + g * (1.0 - s))).astype(BF16)
        dgu[half, :, FL:] = (d * (g * s)).astype(BF16)

    def partial(c, half):
        if c < NC:
            return dot(hid[half], wd[:, c * CW : (c + 1) * CW])
        return dot(dgu[half], wgu[(c - NC) * CW : (c - NC + 1) * CW, :], NT_DIMS)

    def give(c):
        osend[c] = partial(c, 1).astype(BF16)
        rcopy(osend.at[c], orecv.at[c], os_sem.at[c], or_sem.at[c], sibling).start()

    def send_back(c):
        v = partial(c, 0)
        rcopy(osend.at[c], orecv.at[c], os_sem.at[c], or_sem.at[c], sibling).wait_recv()
        rsend[c] = (v + orecv[c].astype(F32)).astype(BF16).reshape(NQ, S2, CW)
        xy_start(rsend.at[c], rrecv.at[c], rs_sem.at[c], rr_sem.at[c])

    for c in loads:
        c.wait()
    for c in xs_list:
        forward(c)
        gate_up(c, 0)
    for c in xs_list:
        forward_wait(c)
        gate_up(c, 1)
    hidden(1)
    for c in xs_list:
        give(c)
    hidden(0)
    for c in xs_list:
        send_back(c)

    for c in dy_list:
        forward(c)
        d_hidden(c, 0)
    for c in dy_list:
        forward_wait(c)
        d_hidden(c, 1)
    d_gate_up(1)
    for c in dy_list:
        give(c)
    d_gate_up(0)
    for c in dy_list:
        send_back(c)

    def combine(c):
        xy_wait(rsend.at[c], rrecv.at[c], rs_sem.at[c], rr_sem.at[c])
        rows = rrecv[c].reshape(R, CW)
        if c < NC:
            part[c] = dot(comb[1], rows) + dot(comb[2], rows)
        else:
            part[c] = dot(comb[0], rows)

    def sums(c, n, down):
        dev = z_down if down else z_up
        m = n - 1 if down else HP + n - 1
        return rcopy(tsend.at[c, m], trecv.at[c, m], ts_sem.at[c], tr_sem.at[c, m], dev)

    def sum_step(c, step):
        for down, hops in ((True, HP), (False, HM)):
            n = hops + 1 - step
            if n < 1:
                continue
            slot = n if down else HP + n
            v = part[c, slot * T : (slot + 1) * T, :]
            if n < hops:
                sums(c, n + 1, down).wait_recv()
                v = v + trecv[c, slot].astype(F32)
            tsend[c, slot - 1] = v.astype(BF16)
            sums(c, n, down).start()

    def finish(c):
        v = part[c, 0:T, :]
        sums(c, 1, True).wait_recv()
        v = v + trecv[c, 0].astype(F32)
        if HM:
            sums(c, 1, False).wait_recv()
            v = v + trecv[c, HP].astype(F32)
        ref = mixed_ref if c < NC else gt_ref
        i = c % NC
        ref[:, i * CW : (i + 1) * CW] = v.astype(BF16)

    def grad_gate_up(i):
        rows = xr[i].reshape(2 * R, CW)
        ggu[i * CW : (i + 1) * CW, :] = dot(rows, dgu[...].reshape(2 * R, 2 * FL), TN_DIMS).astype(BF16)

    def grad_down(i):
        rows = xr[NC + i].reshape(2 * R, CW)
        ggd[:, i * CW : (i + 1) * CW] = dot(hid[...].reshape(2 * R, FL), rows, TN_DIMS).astype(BF16)

    work = [functools.partial(grad_gate_up, i) for i in range(NC)]
    work += [functools.partial(grad_down, i) for i in range(NC)]
    for c in xs_list:
        combine(c)
    for step in range(1, HP + 1):
        for c in xs_list:
            sum_step(c, step)
        if work:
            work.pop(0)()
    for w in work:
        w()
    stores = [
        pltpu.make_async_copy(ggu.at[:, pl.ds(0, FL)], gg_hbm, g_sem.at[0]),
        pltpu.make_async_copy(ggu.at[:, pl.ds(FL, FL)], gu_hbm, g_sem.at[1]),
        pltpu.make_async_copy(ggd, gd_hbm, g_sem.at[2]),
    ]
    for c in stores:
        c.start()
    for c in xs_list:
        finish(c)
    for c in dy_list:
        combine(c)
    for step in range(1, HP + 1):
        for c in dy_list:
            sum_step(c, step)
    for c in dy_list:
        finish(c)

    rest = NQ - 1
    rcopy(zg.at[pl.ds(0, NB - 1)], zg.at[pl.ds(0, NB - 1)], zgs_sem.at[0], zgr_sem.at[0], sibling).wait_send()
    for c in range(2 * NC):
        a = zx.at[c, pl.ds(0, NB - 1)]
        rcopy(a, a, ags_sem.at[c], agr_sem.at[c, 0], sibling).wait_send()
        a = xs.at[c, pl.ds(0, rest)]
        rcopy(a, a, xs_sem.at[c], xr_sem.at[c], sibling).wait_send()
        rcopy(xr.at[c, 0], xr.at[c, 1], fs_sem.at[c], fr_sem.at[c], sibling).wait_send()
        rcopy(osend.at[c], orecv.at[c], os_sem.at[c], or_sem.at[c], sibling).wait_send()
        a = rsend.at[c, pl.ds(0, rest)]
        rcopy(a, a, rs_sem.at[c], rr_sem.at[c], sibling).wait_send()
        rcopy(tsend.at[c], trecv.at[c], ts_sem.at[c], tr_sem.at[c, 0], sibling).wait_send()
    for c in stores:
        c.wait()


def on_device(nx, ny, nz, nc, tokens, upstream, gate_weights, group_choice, pair_pick, w_gate, w_up, w_down):
    T, D = tokens.shape
    FL = w_gate.shape[-1]
    E = nx * ny * nz
    nq, cw, s2 = nx * ny, D // nc, 2 * nz
    R, NT, C2 = nq * s2, nz * T, 2 * nc
    dma = pltpu.SemaphoreType.DMA
    anywhere = pl.BlockSpec(memory_space=pl.ANY)
    vmem = pl.BlockSpec(memory_space=pltpu.VMEM)
    V = pltpu.VMEM
    out = pl.pallas_call(
        functools.partial(kernel, (nx, ny, nz, nc, E)),
        out_shape=(
            jax.ShapeDtypeStruct((T, D), BF16),
            jax.ShapeDtypeStruct((T, D), BF16),
            jax.ShapeDtypeStruct((D, FL), BF16),
            jax.ShapeDtypeStruct((D, FL), BF16),
            jax.ShapeDtypeStruct((FL, D), BF16),
        ),
        in_specs=[vmem] * 5 + [anywhere] * 3,
        out_specs=(vmem, vmem, anywhere, anywhere, anywhere),
        scratch_shapes=[
            V((C2, nz, T, cw), BF16),
            V((nz, T, 2 * E), BF16),
            V((C2, nq, s2, cw), BF16),
            V((C2, 2, nq, s2, cw), BF16),
            V((R, NT), BF16),
            V((3, NT, R), BF16),
            V((R, 128), F32),
            V((D, 2 * FL), BF16),
            V((FL, D), BF16),
            V((2, R, 2 * FL), F32),
            V((2, R, FL), F32),
            V((2, R, FL), BF16),
            V((2, R, 2 * FL), BF16),
            V((C2, R, cw), BF16),
            V((C2, R, cw), BF16),
            V((C2, nq, s2, cw), BF16),
            V((C2, nq, s2, cw), BF16),
            V((C2, NT, cw), F32),
            V((C2, nz - 1, T, cw), BF16),
            V((C2, nz - 1, T, cw), BF16),
            V((D, 2 * FL), BF16),
            V((FL, D), BF16),
            dma((3,)), dma((3,)),
            dma((C2,)), dma((C2, nz - 1)),
            dma((1,)), dma((nz - 1,)),
            dma((C2,)), dma((C2,)),
            dma((C2,)), dma((C2,)),
            dma((C2,)), dma((C2,)),
            dma((C2,)), dma((C2,)),
            dma((C2,)), dma((C2, nz - 1)),
        ],
        compiler_params=pltpu.CompilerParams(
            collective_id=0, has_side_effects=True, vmem_limit_bytes=56 * 1024 * 1024
        ),
    )(
        tokens, upstream, gate_weights, group_choice,
        pair_pick.reshape(T, -1), w_gate[0, 0], w_up[0, 0], w_down[0, 0],
    )
    mixed, grad_tokens, gg, gu, gd = out
    return mixed, grad_tokens, gg[None, None], gu[None, None], gd[None, None]


def solution(mesh):
    ny = mesh.shape["group"]
    nz = mesh.shape["inner"] // (2 * XDIM)
    both = ("group", "inner")
    flat, deep, three = P(both, None), P(both, None, None, None), P(both, None, None)
    return jax.shard_map(
        functools.partial(on_device, XDIM, ny, nz, CHUNKS),
        mesh=mesh,
        in_specs=(flat, flat, flat, flat, three, deep, deep, deep),
        out_specs=(flat, flat, deep, deep, deep),
        check_vma=False,
    )
```

```python
import functools

import jax
import jax.numpy as jnp
from jax import lax
from jax.experimental import pallas as pl
from jax.experimental.pallas import tpu as pltpu
from jax.sharding import PartitionSpec as P

MESH = pl.DeviceIdType.MESH
F32 = jnp.float32
BF16 = jnp.bfloat16

XDIM = 4
CHUNKS = 2

NT_DIMS = (((1,), (1,)), ((), ()))
TN_DIMS = (((0,), (0,)), ((), ()))


def dot(a, b, dims=(((1,), (0,)), ((), ()))):
    return lax.dot_general(a, b, dims, preferred_element_type=F32)


def kernel(
    cfg,
    tok_ref, dy_ref, gw_ref, gc_ref, pp_ref, wg_hbm, wu_hbm, wd_hbm,
    mixed_ref, gt_ref, gg_ref, gu_ref, gd_ref,
    zx, zg, gsrc, xs, xr, amat, comb, wcol, wgu, wd, acc, dh, hid, dgu,
    osend, orecv, rsend, rrecv, part, tsend, trecv,
    w_sem, own_sem, ags_sem, agr_sem, zgs_sem, zgr_sem, xs_sem, xr_sem, fs_sem, fr_sem,
    os_sem, or_sem, rs_sem, rr_sem, ts_sem, tr_sem,
):
    NX, NY, NZ, NC, E = cfg
    NQ = NX * NY
    T, D = tok_ref.shape
    CW = D // NC
    FL = wd.shape[0]
    NB = NZ
    GB = NB // 2
    S2 = 2 * GB
    RG = NQ * S2
    R = 2 * RG
    TG = GB * T
    HP, HM = NZ // 2, NZ - 1 - NZ // 2
    HA = GB // 2
    pairs = gc_ref.shape[0]
    per_group = E // (pairs * 2)
    lz, ln = NZ.bit_length() - 1, NQ.bit_length() - 1
    lt, lg, l2 = T.bit_length() - 1, GB.bit_length() - 1, S2.bit_length() - 1

    y = lax.axis_index("group")
    inner = lax.axis_index("inner")
    core = lax.rem(inner, 2)
    z = lax.rem(lax.div(inner, 2), NZ)
    x = lax.div(inner, 2 * NZ)
    q_me = y * NX + x

    def place(px, pz, pc):
        return (px * NZ + pz) * 2 + pc

    def z_peer(d):
        return (y, place(x, lax.rem(z + d, NZ), core))

    z_up, z_down = z_peer(1), z_peer(NZ - 1)
    sibling = (y, place(x, z, 1 - core))

    offsets = [(i, j) for i in range(NX) for j in range(NY) if i or j]
    offsets.sort(key=lambda o: (not (o[0] and o[1]), min(o[0], NX - o[0]) + min(o[1], NY - o[1])))
    plane = []
    for i, j in offsets:
        tx, ty = lax.rem(x + i, NX), lax.rem(y + j, NY)
        plane.append((ty * NX + tx, (ty, place(tx, z, core))))

    def rcopy(src, dst, ssem, rsem, dev):
        return pltpu.make_async_remote_copy(
            src_ref=src, dst_ref=dst, send_sem=ssem, recv_sem=rsem, device_id=dev, device_id_type=MESH
        )

    barrier = pltpu.get_barrier_semaphore()
    partners = [z_peer(d) for d in range(1, NZ)] + [dev for _, dev in plane] + [sibling]
    for dev in partners:
        pl.semaphore_signal(barrier, inc=1, device_id=dev, device_id_type=MESH)

    loads = [
        pltpu.make_async_copy(wg_hbm, wgu.at[:, pl.ds(0, FL)], w_sem.at[0]),
        pltpu.make_async_copy(wu_hbm, wgu.at[:, pl.ds(FL, FL)], w_sem.at[1]),
        pltpu.make_async_copy(wd_hbm, wd, w_sem.at[2]),
    ]
    for c in loads:
        c.start()

    row = lax.broadcasted_iota(jnp.int32, (E, T), 0)
    table = jnp.zeros((E, T), F32)
    for k in range(2 * pairs):
        ids = gc_ref[k // 2 : k // 2 + 1, :] * per_group + pp_ref[k // 2, k % 2 : k % 2 + 1, :]
        ids = ((ids & (NZ - 1)) << ln) + (ids >> lz)
        table = table + jnp.where(ids == row, gw_ref[k : k + 1, :], 0.0)
    hi = table.astype(BF16)
    gsrc[:, 0:NQ, :] = hi.reshape(NZ, NQ, T)
    gsrc[:, NQ:, :] = (table - hi.astype(F32)).astype(BF16).reshape(NZ, NQ, T)
    for c in range(NC):
        zx[c, 0] = tok_ref[:, c * CW : (c + 1) * CW]
        zx[NC + c, 0] = dy_ref[:, c * CW : (c + 1) * CW]

    pl.semaphore_wait(barrier, len(partners))

    def spot(h, down):
        return 0 if h == 0 else (2 * h if down else 2 * h - 1)

    tables = []
    for d in range(1, NZ):
        at = spot(d, False) if d <= HP else spot(NZ - d, True)
        dev = z_peer(d)
        tables.append(rcopy(gsrc.at[lax.rem(z + d, NZ)], zg.at[at], zgs_sem.at[0], zgr_sem.at[at - 1], dev))
    own_table = pltpu.make_async_copy(gsrc.at[z], zg.at[0], own_sem.at[0])

    def ag(c, h):
        out = [rcopy(zx.at[c, spot(h - 1, False)], zx.at[c, spot(h, False)], ags_sem.at[c],
                     agr_sem.at[c, spot(h, False) - 1], z_up)]
        if h <= HM:
            out.append(rcopy(zx.at[c, spot(h - 1, True)], zx.at[c, spot(h, True)], ags_sem.at[c],
                             agr_sem.at[c, spot(h, True) - 1], z_down))
        return out

    def ag_send(c, h):
        for d in ag(c, h):
            d.start()

    def ag_wait(c, h):
        for d in ag(c, h):
            d.wait_recv()

    def rows_at(q):
        return pl.ds(pl.multiple_of(q * S2, S2), S2)

    def xy_start(src, dst, ssem, rsem):
        for tq, dev in plane:
            rcopy(src.at[rows_at(tq)], dst.at[rows_at(q_me)], ssem, rsem, dev).start()
        pltpu.make_async_copy(src.at[rows_at(q_me)], dst.at[rows_at(q_me)], rsem).start()

    def xy_wait(dst, rsem):
        rcopy(dst, dst, rsem, rsem, sibling).wait_recv()

    def slot_tables(g):
        span = slice(g * GB, (g + 1) * GB)
        whi = zg[span, 0:NQ, :].reshape(GB * NQ, T).astype(F32)
        wlo = zg[span, NQ:, :].reshape(GB * NQ, T).astype(F32)
        routed = whi > 0.0
        i0 = lax.broadcasted_iota(jnp.int32, (T, T), 0)
        i1 = lax.broadcasted_iota(jnp.int32, (T, T), 1)
        earlier = jnp.where(i0 < i1, 1.0, 0.0).astype(BF16)
        rank = dot(jnp.where(routed, 1.0, 0.0).astype(BF16), earlier)
        first = jnp.where(routed & (rank < 0.5), 1.0, 0.0)
        second = jnp.where(routed & (rank > 0.5) & (rank < 1.5), 1.0, 0.0)
        k0 = lax.broadcasted_iota(jnp.int32, (2 * GB * NQ, TG), 0)
        k1 = lax.broadcasted_iota(jnp.int32, (2 * GB * NQ, TG), 1)
        block = ((k0 >> ln) & (GB - 1)) == (k1 >> lt)

        def spread(a, b):
            v = jnp.concatenate([a, b], axis=0)
            return jnp.where(block, jnp.concatenate([v] * GB, axis=1), 0.0).astype(BF16)

        r = lax.broadcasted_iota(jnp.int32, (RG, 2 * GB * NQ), 0)
        k = lax.broadcasted_iota(jnp.int32, (RG, 2 * GB * NQ), 1)
        same = ((r >> l2) == (k & (NQ - 1))) & (((r >> 1) & (GB - 1)) == ((k >> ln) & (GB - 1)))
        sel = jnp.where(same & ((r & 1) == (k >> (ln + lg))), 1.0, 0.0).astype(BF16)
        ones = dot(sel, spread(first, second))
        his = dot(sel, spread(first * whi, second * whi))
        los = dot(sel, spread(first * wlo, second * wlo))
        amat[g] = ones.astype(BF16)
        wcol[g] = jnp.broadcast_to(jnp.sum(his + los, axis=1, keepdims=True), (RG, 128))
        return ones, his, los

    def comb_tables(g, made):
        for n, v in enumerate(made):
            comb[g, n] = jnp.transpose(v).astype(BF16)

    def gather(c, g):
        rows = dot(amat[g], zx[c, g * GB : (g + 1) * GB].reshape(TG, CW))
        if c >= NC:
            rows = rows * wcol[g, :, 0:1]
        xs[c, g] = rows.astype(BF16)
        xy_start(xs.at[c, g], xr.at[c, 0, g], xs_sem.at[c, g], xr_sem.at[c, g])

    def forward(c, g):
        xy_wait(xr.at[c, 0, g], xr_sem.at[c, g])
        rcopy(xr.at[c, 0, g], xr.at[c, 1, g], fs_sem.at[c, g], fr_sem.at[c, g], sibling).start()

    def forward_wait(c, g):
        rcopy(xr.at[c, 0, g], xr.at[c, 1, g], fs_sem.at[c, g], fr_sem.at[c, g], sibling).wait_recv()

    def rows_of(c, half):
        return xr[c, half].reshape(R, CW)

    def gate_up(c, half):
        v = dot(rows_of(c, half), wgu[c * CW : (c + 1) * CW, :])
        acc[half] = v if c == 0 else acc[half] + v

    def hidden(half):
        v = acc[half]
        g, u = v[:, 0:FL], v[:, FL:]
        hid[half] = (g * jax.nn.sigmoid(g) * u).astype(BF16)

    def d_hidden(c, half):
        cols = slice((c - NC) * CW, (c - NC + 1) * CW)
        v = dot(rows_of(c, half), wd[:, cols], NT_DIMS)
        dh[half] = v if c == NC else dh[half] + v

    def d_gate_up(half):
        v = acc[half]
        g, u = v[:, 0:FL], v[:, FL:]
        s = jax.nn.sigmoid(g)
        d = dh[half]
        dgu[half, :, 0:FL] = (d * u * s * (1.0 + g * (1.0 - s))).astype(BF16)
        dgu[half, :, FL:] = (d * (g * s)).astype(BF16)

    def partial(c, half):
        if c < NC:
            return dot(hid[half], wd[:, c * CW : (c + 1) * CW])
        return dot(dgu[half], wgu[(c - NC) * CW : (c - NC + 1) * CW, :], NT_DIMS)

    def give(c):
        osend[c] = partial(c, 1).astype(BF16)
        rcopy(osend.at[c], orecv.at[c], os_sem.at[c], or_sem.at[c], sibling).start()

    def back_start(c, g):
        xy_start(rsend.at[c, g], rrecv.at[c, g], rs_sem.at[c, g], rr_sem.at[c, g])

    def send_back(c):
        v = partial(c, 0)
        rcopy(osend.at[c], orecv.at[c], os_sem.at[c], or_sem.at[c], sibling).wait_recv()
        rsend[c] = (v + orecv[c].astype(F32)).astype(BF16).reshape(2, RG, CW)
        back_start(c, 1)

    def combine(c, g):
        xy_wait(rrecv.at[c, g], rr_sem.at[c, g])
        rows = rrecv[c, g]
        if c < NC:
            part[c, g] = dot(comb[g, 1], rows) + dot(comb[g, 2], rows)
        else:
            part[c, g] = dot(comb[g, 0], rows)

    def block_sum(c, at):
        lo = (at % GB) * T
        return part[c, at // GB, lo : lo + T, :]

    def sums(c, n, down):
        at = spot(n, not down)
        dev = z_down if down else z_up
        return rcopy(tsend.at[c, at - 1], trecv.at[c, at - 1], ts_sem.at[c], tr_sem.at[c, at - 1], dev)

    def sum_step(c, n):
        for down, hops in ((True, HP), (False, HM)):
            if n > hops:
                continue
            at = spot(n, not down)
            v = block_sum(c, at)
            if n < hops:
                sums(c, n + 1, down).wait_recv()
                v = v + trecv[c, spot(n + 1, not down) - 1].astype(F32)
            tsend[c, at - 1] = v.astype(BF16)
            sums(c, n, down).start()

    def finish(c):
        v = block_sum(c, 0)
        for down, hops in ((True, HP), (False, HM)):
            if hops:
                sums(c, 1, down).wait_recv()
                v = v + trecv[c, spot(1, not down) - 1].astype(F32)
        ref = mixed_ref if c < NC else gt_ref
        i = c % NC
        ref[:, i * CW : (i + 1) * CW] = v.astype(BF16)

    def grad_gate_up(i):
        rows = xr[i].reshape(2 * R, CW)
        v = dot(rows, dgu[...].reshape(2 * R, 2 * FL), TN_DIMS).astype(BF16)
        gg_ref[i * CW : (i + 1) * CW, :] = v[:, 0:FL]
        gu_ref[i * CW : (i + 1) * CW, :] = v[:, FL:]

    def grad_down(i):
        rows = xr[NC + i].reshape(2 * R, CW)
        gd_ref[:, i * CW : (i + 1) * CW] = dot(hid[...].reshape(2 * R, FL), rows, TN_DIMS).astype(BF16)

    xs_list = list(range(NC))
    dy_list = list(range(NC, 2 * NC))
    for d in tables:
        d.start()
    own_table.start()
    for c in xs_list:
        ag_send(c, 1)
    own_table.wait()
    for d in tables:
        d.wait_recv()
    made = [slot_tables(0)]

    def ring_step(chunks, h):
        for c in chunks:
            ag_wait(c, h)
            if h < HP:
                ag_send(c, h + 1)
            if h == HA:
                gather(c, 0)
            if h == HP:
                gather(c, 1)

    for h in range(1, HP + 1):
        if h == HP:
            for c in dy_list:
                ag_send(c, 1)
        ring_step(xs_list, h)
        if h == 1:
            made.append(slot_tables(1))
    for g in range(2):
        comb_tables(g, made[g])
    ring_step(dy_list, 1)
    for c in xs_list:
        forward(c, 0)
    for h in range(2, HP):
        ring_step(dy_list, h)
        if h == 2:
            for c in loads:
                c.wait()
            for c in xs_list:
                forward(c, 1)
                gate_up(c, 0)
    if HP <= 2:
        for c in loads:
            c.wait()
        for c in xs_list:
            forward(c, 1)
            gate_up(c, 0)
    for c in xs_list:
        for g in range(2):
            forward_wait(c, g)
        gate_up(c, 1)
    ring_step(dy_list, HP)
    hidden(1)
    for c in xs_list:
        give(c)
    hidden(0)
    for c in xs_list:
        send_back(c)
    for c in xs_list:
        back_start(c, 0)

    for g in range(2):
        for c in dy_list:
            forward(c, g)
    for c in dy_list:
        d_hidden(c, 0)
    for c in dy_list:
        for g in range(2):
            forward_wait(c, g)
        d_hidden(c, 1)
    d_gate_up(1)
    for c in dy_list:
        give(c)
    d_gate_up(0)
    for c in dy_list:
        send_back(c)
    for c in dy_list:
        back_start(c, 0)

    work = []
    for i in range(NC):
        work.append(functools.partial(grad_down, i))
        work.append(functools.partial(grad_gate_up, i))

    def sum_chain(chunks):
        for c in chunks:
            combine(c, 1)
            sum_step(c, HP)
        for n in range(HP - 1, 0, -1):
            if n == HA:
                for c in chunks:
                    combine(c, 0)
            if work:
                work.pop(0)()
            for c in chunks:
                sum_step(c, n)
        if work:
            work.pop(0)()
        for c in chunks:
            finish(c)

    sum_chain(xs_list)
    while work:
        work.pop(0)()
    sum_chain(dy_list)

    a = zg.at[pl.ds(0, NB - 1)]
    rcopy(a, a, zgs_sem.at[0], zgr_sem.at[0], sibling).wait_send()
    rest = pl.ds(0, RG - S2)
    for c in range(2 * NC):
        a = zx.at[c, pl.ds(0, NB - 1)]
        rcopy(a, a, ags_sem.at[c], agr_sem.at[c, 0], sibling).wait_send()
        for g in range(2):
            a = xs.at[c, g, rest]
            rcopy(a, a, xs_sem.at[c, g], xr_sem.at[c, g], sibling).wait_send()
            rcopy(xr.at[c, 0, g], xr.at[c, 1, g], fs_sem.at[c, g], fr_sem.at[c, g], sibling).wait_send()
            a = rsend.at[c, g, rest]
            rcopy(a, a, rs_sem.at[c, g], rr_sem.at[c, g], sibling).wait_send()
        rcopy(osend.at[c], orecv.at[c], os_sem.at[c], or_sem.at[c], sibling).wait_send()
        rcopy(tsend.at[c], trecv.at[c], ts_sem.at[c], tr_sem.at[c, 0], sibling).wait_send()


def write_out(*refs):
    n = (len(refs) - 1) // 2
    copies = [pltpu.make_async_copy(refs[i], refs[n + i], refs[-1].at[i]) for i in range(n)]
    for c in copies:
        c.start()
    for c in copies:
        c.wait()


def on_device(nx, ny, nz, nc, tokens, upstream, gate_weights, group_choice, pair_pick, w_gate, w_up, w_down):
    T, D = tokens.shape
    FL = w_gate.shape[-1]
    E = nx * ny * nz
    nq, cw, gb = nx * ny, D // nc, nz // 2
    rg, tg, C2 = nq * 2 * gb, gb * T, 2 * nc
    R = 2 * rg
    dma = pltpu.SemaphoreType.DMA
    anywhere = pl.BlockSpec(memory_space=pl.ANY)
    vmem = pl.BlockSpec(memory_space=pltpu.VMEM)
    V = pltpu.VMEM
    shapes = [(T, D), (T, D), (D, FL), (D, FL), (FL, D)]
    held = pl.pallas_call(
        functools.partial(kernel, (nx, ny, nz, nc, E)),
        out_shape=[V(s, BF16) for s in shapes],
        in_specs=[vmem] * 5 + [anywhere] * 3,
        out_specs=[vmem] * 5,
        scratch_shapes=[
            V((C2, nz, T, cw), BF16),
            V((nz, 2 * nq, T), BF16),
            V((nz, 2 * nq, T), BF16),
            V((C2, 2, rg, cw), BF16),
            V((C2, 2, 2, rg, cw), BF16),
            V((2, rg, tg), BF16),
            V((2, 3, tg, rg), BF16),
            V((2, rg, 128), F32),
            V((D, 2 * FL), BF16),
            V((FL, D), BF16),
            V((2, R, 2 * FL), F32),
            V((2, R, FL), F32),
            V((2, R, FL), BF16),
            V((2, R, 2 * FL), BF16),
            V((C2, R, cw), BF16),
            V((C2, R, cw), BF16),
            V((C2, 2, rg, cw), BF16),
            V((C2, 2, rg, cw), BF16),
            V((C2, 2, tg, cw), F32),
            V((C2, nz - 1, T, cw), BF16),
            V((C2, nz - 1, T, cw), BF16),
            dma((3,)), dma((1,)),
            dma((C2,)), dma((C2, nz - 1)),
            dma((1,)), dma((nz - 1,)),
            dma((C2, 2)), dma((C2, 2)),
            dma((C2, 2)), dma((C2, 2)),
            dma((C2,)), dma((C2,)),
            dma((C2, 2)), dma((C2, 2)),
            dma((C2,)), dma((C2, nz - 1)),
        ],
        compiler_params=pltpu.CompilerParams(
            collective_id=0, has_side_effects=True, vmem_limit_bytes=48 * 1024 * 1024
        ),
    )(
        tokens, upstream, gate_weights.T, group_choice.T,
        pair_pick.transpose(1, 2, 0), w_gate[0, 0], w_up[0, 0], w_down[0, 0],
    )
    mixed, grad_tokens, gg, gu, gd = pl.pallas_call(
        write_out,
        out_shape=[jax.ShapeDtypeStruct(s, BF16) for s in shapes],
        in_specs=[vmem] * 5,
        out_specs=[anywhere] * 5,
        scratch_shapes=[dma((5,))],
    )(*held)
    return mixed, grad_tokens, gg[None, None], gu[None, None], gd[None, None]


def solution(mesh):
    ny = mesh.shape["group"]
    nz = mesh.shape["inner"] // (2 * XDIM)
    both = ("group", "inner")
    flat, deep, three = P(both, None), P(both, None, None, None), P(both, None, None)
    return jax.shard_map(
        functools.partial(on_device, XDIM, ny, nz, CHUNKS),
        mesh=mesh,
        in_specs=(flat, flat, flat, flat, three, deep, deep, deep),
        out_specs=(flat, flat, deep, deep, deep),
        check_vma=False,
    )
```

```python
import functools

import jax
import jax.numpy as jnp
from jax import lax
from jax.experimental import pallas as pl
from jax.experimental.pallas import tpu as pltpu
from jax.sharding import PartitionSpec as P

MESH = pl.DeviceIdType.MESH
F32 = jnp.float32
BF16 = jnp.bfloat16

THR = 0
STHR = 0
BTHR = 0
DYAT = 2
EARLY = 1
XDIM = 4
CHUNKS = 2

NT_DIMS = (((1,), (1,)), ((), ()))
TN_DIMS = (((0,), (0,)), ((), ()))


def dot(a, b, dims=(((1,), (0,)), ((), ()))):
    return lax.dot_general(a, b, dims, preferred_element_type=F32)


def kernel(
    cfg,
    tok_hbm, dy_hbm, gw_hbm, gc_hbm, pp_hbm, wg_hbm, wu_hbm, wd_hbm,
    mixed_ref, gt_ref, gg_ref, gu_ref, gd_ref,
    gw_ref, gc_ref, pp_ref, zx, zg, gsrc, xs, xr, amat, comb, wcol, wgu, wd, acc, dh, hid, dgu,
    osend, orecv, rsend, rrecv, part, tsend, trecv,
    w_sem, i_sem, own_sem, ags_sem, agr_sem, zgs_sem, zgr_sem, xs_sem, xr_sem, fs_sem, fr_sem,
    os_sem, or_sem, rs_sem, rr_sem, ts_sem, tr_sem,
):
    NX, NY, NZ, NC, E = cfg
    NQ = NX * NY
    T, D = tok_hbm.shape
    CW = D // NC
    FL = wd.shape[0]
    NB = NZ
    GB = NB // 2
    S2 = 2 * GB
    RG = NQ * S2
    R = 2 * RG
    TG = GB * T
    HP, HM = NZ // 2, NZ - 1 - NZ // 2
    HA = GB // 2
    pairs = gc_ref.shape[0]
    per_group = E // (pairs * 2)
    lz, ln = NZ.bit_length() - 1, NQ.bit_length() - 1
    lt, lg, l2 = T.bit_length() - 1, GB.bit_length() - 1, S2.bit_length() - 1

    y = lax.axis_index("group")
    inner = lax.axis_index("inner")
    core = lax.rem(inner, 2)
    z = lax.rem(lax.div(inner, 2), NZ)
    x = lax.div(inner, 2 * NZ)
    q_me = y * NX + x

    def place(px, pz, pc):
        return (px * NZ + pz) * 2 + pc

    def z_peer(d):
        return (y, place(x, lax.rem(z + d, NZ), core))

    z_up, z_down = z_peer(1), z_peer(NZ - 1)
    sibling = (y, place(x, z, 1 - core))

    offsets = [(i, j) for i in range(NX) for j in range(NY) if i or j]
    offsets.sort(key=lambda o: (not (o[0] and o[1]), min(o[0], NX - o[0]) + min(o[1], NY - o[1])))
    plane = []
    for i, j in offsets:
        tx, ty = lax.rem(x + i, NX), lax.rem(y + j, NY)
        plane.append((ty * NX + tx, (ty, place(tx, z, core))))

    def rcopy(src, dst, ssem, rsem, dev):
        return pltpu.make_async_remote_copy(
            src_ref=src, dst_ref=dst, send_sem=ssem, recv_sem=rsem, device_id=dev, device_id_type=MESH
        )

    small = [
        pltpu.make_async_copy(a, b, i_sem.at[i])
        for i, (a, b) in enumerate(((gw_hbm, gw_ref), (gc_hbm, gc_ref), (pp_hbm, pp_ref)))
    ]
    rows_in = [
        pltpu.make_async_copy(h.at[:, pl.ds(c * CW, CW)], zx.at[n * NC + c, 0], i_sem.at[3 + n * NC + c])
        for n, h in enumerate((tok_hbm, dy_hbm))
        for c in range(NC)
    ]
    for c in small + rows_in:
        c.start()
    barrier = pltpu.get_barrier_semaphore()
    partners = [z_peer(d) for d in range(1, NZ)] + [dev for _, dev in plane] + [sibling]
    for dev in partners:
        pl.semaphore_signal(barrier, inc=1, device_id=dev, device_id_type=MESH)

    loads = [
        pltpu.make_async_copy(wg_hbm, wgu.at[:, pl.ds(0, FL)], w_sem.at[0]),
        pltpu.make_async_copy(wu_hbm, wgu.at[:, pl.ds(FL, FL)], w_sem.at[1]),
        pltpu.make_async_copy(wd_hbm, wd, w_sem.at[2]),
    ]
    for c in loads:
        c.start()
    for c in small:
        c.wait()

    row = lax.broadcasted_iota(jnp.int32, (E, T), 0)
    table = jnp.zeros((E, T), F32)
    for k in range(2 * pairs):
        ids = gc_ref[k // 2 : k // 2 + 1, :] * per_group + pp_ref[k // 2, k % 2 : k % 2 + 1, :]
        ids = ((ids & (NZ - 1)) << ln) + (ids >> lz)
        table = table + jnp.where(ids == row, gw_ref[k : k + 1, :], 0.0)
    hi = table.astype(BF16)
    gsrc[:, 0:NQ, :] = hi.reshape(NZ, NQ, T)
    gsrc[:, NQ:, :] = (table - hi.astype(F32)).astype(BF16).reshape(NZ, NQ, T)
    for c in rows_in:
        c.wait()
    pl.semaphore_wait(barrier, len(partners))

    def spot(h, down):
        return 0 if h == 0 else (2 * h if down else 2 * h - 1)

    tables = []
    for d in range(1, NZ):
        at = spot(d, False) if d <= HP else spot(NZ - d, True)
        dev = z_peer(d)
        tables.append(rcopy(gsrc.at[lax.rem(z + d, NZ)], zg.at[at], zgs_sem.at[0], zgr_sem.at[at - 1], dev))
    own_table = pltpu.make_async_copy(gsrc.at[z], zg.at[0], own_sem.at[0])

    flying = {}

    def later(key, copies):
        flying[key] = copies

    def sent(key):
        for d in flying.pop(key):
            d.wait_send()

    def ag(c, h):
        out = []
        for down, dev in ((False, z_up), (True, z_down))[: 1 + (h <= HM)]:
            at = spot(h, down)
            out.append(rcopy(zx.at[c, spot(h - 1, down)], zx.at[c, at], ags_sem.at[c, at - 1],
                             agr_sem.at[c, at - 1], dev))
        return out

    def ag_send(c, h, arrived=()):
        copies = ag(c, h)
        for i, d in enumerate(copies):
            if i < len(arrived):
                arrived[i].wait_recv()
            d.start()
        for d in arrived[len(copies) :]:
            d.wait_recv()
        later(("ring", c, h), copies)

    def ring_start(chunks):
        for c in chunks:
            ag_send(c, 1)
            if THR and c != chunks[-1]:
                sent(("ring", c, 1))

    def ag_wait(c, h):
        for d in ag(c, h):
            d.wait_recv()

    def rows_at(q):
        return pl.ds(pl.multiple_of(q * S2, S2), S2)

    def xy_start(key, src, dst, ssem, rsem):
        for tq, dev in plane:
            rcopy(src.at[rows_at(tq)], dst.at[rows_at(q_me)], ssem, rsem, dev).start()
        pltpu.make_async_copy(src.at[rows_at(q_me)], dst.at[rows_at(q_me)], rsem).start()
        away = src.at[pl.ds(0, RG - S2)]
        later(key, [rcopy(away, away, ssem, rsem, sibling)])

    def xy_wait(dst, rsem):
        rcopy(dst, dst, rsem, rsem, sibling).wait_recv()

    def slot_tables(g):
        span = slice(g * GB, (g + 1) * GB)
        whi = zg[span, 0:NQ, :].reshape(GB * NQ, T).astype(F32)
        wlo = zg[span, NQ:, :].reshape(GB * NQ, T).astype(F32)
        routed = whi > 0.0
        i0 = lax.broadcasted_iota(jnp.int32, (T, T), 0)
        i1 = lax.broadcasted_iota(jnp.int32, (T, T), 1)
        earlier = jnp.where(i0 < i1, 1.0, 0.0).astype(BF16)
        rank = dot(jnp.where(routed, 1.0, 0.0).astype(BF16), earlier)
        first = jnp.where(routed & (rank < 0.5), 1.0, 0.0)
        second = jnp.where(routed & (rank > 0.5) & (rank < 1.5), 1.0, 0.0)
        k0 = lax.broadcasted_iota(jnp.int32, (2 * GB * NQ, TG), 0)
        k1 = lax.broadcasted_iota(jnp.int32, (2 * GB * NQ, TG), 1)
        block = ((k0 >> ln) & (GB - 1)) == (k1 >> lt)

        def spread(a, b):
            v = jnp.concatenate([a, b], axis=0)
            return jnp.where(block, jnp.concatenate([v] * GB, axis=1), 0.0).astype(BF16)

        r = lax.broadcasted_iota(jnp.int32, (RG, 2 * GB * NQ), 0)
        k = lax.broadcasted_iota(jnp.int32, (RG, 2 * GB * NQ), 1)
        same = ((r >> l2) == (k & (NQ - 1))) & (((r >> 1) & (GB - 1)) == ((k >> ln) & (GB - 1)))
        sel = jnp.where(same & ((r & 1) == (k >> (ln + lg))), 1.0, 0.0).astype(BF16)
        ones = dot(sel, spread(first, second))
        his = dot(sel, spread(first * whi, second * whi))
        los = dot(sel, spread(first * wlo, second * wlo))
        amat[g] = ones.astype(BF16)
        wcol[g] = jnp.broadcast_to(jnp.sum(his + los, axis=1, keepdims=True), (RG, 128))
        return ones, his, los

    def comb_tables(g, made):
        for n, v in enumerate(made):
            comb[g, n] = jnp.transpose(v).astype(BF16)

    def gather(c, g):
        rows = dot(amat[g], zx[c, g * GB : (g + 1) * GB].reshape(TG, CW))
        if c >= NC:
            rows = rows * wcol[g, :, 0:1]
        xs[c, g] = rows.astype(BF16)
        xy_start(("out", c, g), xs.at[c, g], xr.at[c, 0, g], xs_sem.at[c, g], xr_sem.at[c, g])

    def forward(c, g):
        xy_wait(xr.at[c, 0, g], xr_sem.at[c, g])
        d = rcopy(xr.at[c, 0, g], xr.at[c, 1, g], fs_sem.at[c, g], fr_sem.at[c, g], sibling)
        d.start()
        later(("pass", c, g), [d])

    def forward_wait(c, g):
        rcopy(xr.at[c, 0, g], xr.at[c, 1, g], fs_sem.at[c, g], fr_sem.at[c, g], sibling).wait_recv()

    def rows_of(c, half):
        return xr[c, half].reshape(R, CW)

    def gate_up(c, half):
        v = dot(rows_of(c, half), wgu[c * CW : (c + 1) * CW, :])
        acc[half] = v if c == 0 else acc[half] + v

    def hidden(half):
        v = acc[half]
        g, u = v[:, 0:FL], v[:, FL:]
        hid[half] = (g * jax.nn.sigmoid(g) * u).astype(BF16)

    def d_hidden(c, half):
        cols = slice((c - NC) * CW, (c - NC + 1) * CW)
        v = dot(rows_of(c, half), wd[:, cols], NT_DIMS)
        dh[half] = v if c == NC else dh[half] + v

    def d_gate_up(half):
        v = acc[half]
        g, u = v[:, 0:FL], v[:, FL:]
        s = jax.nn.sigmoid(g)
        d = dh[half]
        dgu[half, :, 0:FL] = (d * u * s * (1.0 + g * (1.0 - s))).astype(BF16)
        dgu[half, :, FL:] = (d * (g * s)).astype(BF16)

    def partial(c, half):
        if c < NC:
            return dot(hid[half], wd[:, c * CW : (c + 1) * CW])
        return dot(dgu[half], wgu[(c - NC) * CW : (c - NC + 1) * CW, :], NT_DIMS)

    def give(c):
        osend[c] = partial(c, 1).astype(BF16)
        d = rcopy(osend.at[c], orecv.at[c], os_sem.at[c], or_sem.at[c], sibling)
        d.start()
        later(("give", c), [d])

    def back_start(c, g):
        xy_start(("back", c, g), rsend.at[c, g], rrecv.at[c, g], rs_sem.at[c, g], rr_sem.at[c, g])

    def send_back(c):
        v = partial(c, 0)
        rcopy(osend.at[c], orecv.at[c], os_sem.at[c], or_sem.at[c], sibling).wait_recv()
        rsend[c] = (v + orecv[c].astype(F32)).astype(BF16).reshape(2, RG, CW)
        back_start(c, 1)

    def combine(c, g):
        xy_wait(rrecv.at[c, g], rr_sem.at[c, g])
        rows = rrecv[c, g]
        if c < NC:
            part[c, g] = dot(comb[g, 1], rows) + dot(comb[g, 2], rows)
        else:
            part[c, g] = dot(comb[g, 0], rows)

    def block_sum(c, at):
        lo = (at % GB) * T
        return part[c, at // GB, lo : lo + T, :]

    def sums(c, n, down):
        at = spot(n, not down)
        dev = z_down if down else z_up
        return rcopy(tsend.at[c, at - 1], trecv.at[c, at - 1], ts_sem.at[c, at - 1], tr_sem.at[c, at - 1], dev)

    def sum_step(c, n):
        copies = []
        for down, hops in ((True, HP), (False, HM)):
            if n > hops:
                continue
            at = spot(n, not down)
            v = block_sum(c, at)
            if n < hops:
                sums(c, n + 1, down).wait_recv()
                v = v + trecv[c, spot(n + 1, not down) - 1].astype(F32)
            tsend[c, at - 1] = v.astype(BF16)
            copies.append(sums(c, n, down))
            copies[-1].start()
        later(("sum", c, n), copies)

    def finish(c):
        v = block_sum(c, 0)
        for down, hops in ((True, HP), (False, HM)):
            if hops:
                sums(c, 1, down).wait_recv()
                v = v + trecv[c, spot(1, not down) - 1].astype(F32)
        ref = mixed_ref if c < NC else gt_ref
        i = c % NC
        ref[:, i * CW : (i + 1) * CW] = v.astype(BF16)

    def grad_gate_up(i):
        rows = xr[i].reshape(2 * R, CW)
        v = dot(rows, dgu[...].reshape(2 * R, 2 * FL), TN_DIMS).astype(BF16)
        gg_ref[i * CW : (i + 1) * CW, :] = v[:, 0:FL]
        gu_ref[i * CW : (i + 1) * CW, :] = v[:, FL:]

    def grad_down(i):
        rows = xr[NC + i].reshape(2 * R, CW)
        gd_ref[:, i * CW : (i + 1) * CW] = dot(hid[...].reshape(2 * R, FL), rows, TN_DIMS).astype(BF16)

    xs_list = list(range(NC))
    dy_list = list(range(NC, 2 * NC))
    for d in tables:
        d.start()
    own_table.start()
    gone = zg.at[pl.ds(0, NB - 1)]
    later("tables", [rcopy(gone, gone, zgs_sem.at[0], zgr_sem.at[0], sibling)])
    ring_start(xs_list)
    own_table.wait()
    for d in tables:
        d.wait_recv()
    made = [slot_tables(0)]

    def ring_step(chunks, h):
        for c in chunks:
            if h < HP:
                ag_send(c, h + 1, ag(c, h))
            else:
                ag_wait(c, h)
            if h == HA:
                gather(c, 0)
            if h == HP:
                gather(c, 1)

    for h in range(1, HP + 1):
        ring_step(xs_list, h)
        if h == DYAT:
            ring_start(dy_list)
        if h == 1:
            made.append(slot_tables(1))
        if EARLY and h > DYAT:
            ring_step(dy_list, h - DYAT)
    for g in range(2):
        comb_tables(g, made[g])
    first_dy = max(HP - DYAT, 0) + 1 if EARLY else 1
    for h in range(first_dy, HP):
        ring_step(dy_list, h)
        if h == max(first_dy, 1):
            for c in xs_list:
                forward(c, 0)
    for c in loads:
        c.wait()
    for c in xs_list:
        forward(c, 1)
        gate_up(c, 0)
    ring_step(dy_list, HP)
    for c in xs_list:
        for g in range(2):
            forward_wait(c, g)
        gate_up(c, 1)
    hidden(1)
    for c in xs_list:
        give(c)
    hidden(0)
    for c in xs_list:
        send_back(c)
    if not BTHR:
        for c in xs_list:
            back_start(c, 0)

    for c in dy_list:
        forward(c, 0)
    if BTHR:
        for c in xs_list:
            sent(("back", c, 1))
            back_start(c, 0)
    for c in dy_list:
        forward(c, 1)
        d_hidden(c, 0)
    for c in dy_list:
        for g in range(2):
            forward_wait(c, g)
        d_hidden(c, 1)
    d_gate_up(1)
    for c in dy_list:
        give(c)
    d_gate_up(0)
    for c in dy_list:
        send_back(c)
    if not BTHR:
        for c in dy_list:
            back_start(c, 0)

    def sum_start(chunks):
        for c in chunks:
            combine(c, 1)
            sum_step(c, HP)
            if STHR and c != chunks[-1]:
                sent(("sum", c, HP))

    def sum_steps(chunks, n):
        for c in chunks:
            if n == HA:
                combine(c, 0)
            sum_step(c, n)

    sum_start(xs_list)
    grad_down(0)
    for n in range(HP - 1, HA, -1):
        sum_steps(xs_list, n)
    if BTHR:
        for c in dy_list:
            sent(("back", c, 1))
            back_start(c, 0)
    for i in range(1, NC):
        grad_down(i)
    sum_steps(xs_list, HA)
    grad_gate_up(0)
    for n in range(HA - 1, 0, -1):
        sum_steps(xs_list, n)
    sum_start(dy_list)
    for c in xs_list:
        finish(c)
    for i in range(1, NC):
        grad_gate_up(i)
    for n in range(HP - 1, 0, -1):
        sum_steps(dy_list, n)
    for c in dy_list:
        finish(c)

    for key in list(flying):
        sent(key)


def write_out(*refs):
    n = (len(refs) - 1) // 2
    copies = [pltpu.make_async_copy(refs[i], refs[n + i], refs[-1].at[i]) for i in range(n)]
    for c in copies:
        c.start()
    for c in copies:
        c.wait()


def on_device(nx, ny, nz, nc, tokens, upstream, gate_weights, group_choice, pair_pick, w_gate, w_up, w_down):
    T, D = tokens.shape
    FL = w_gate.shape[-1]
    E = nx * ny * nz
    nq, cw, gb = nx * ny, D // nc, nz // 2
    rg, tg, C2 = nq * 2 * gb, gb * T, 2 * nc
    R = 2 * rg
    pairs = group_choice.shape[1]
    dma = pltpu.SemaphoreType.DMA
    anywhere = pl.BlockSpec(memory_space=pltpu.HBM)
    vmem = pl.BlockSpec(memory_space=pltpu.VMEM)
    V = pltpu.VMEM
    shapes = [(T, D), (T, D), (D, FL), (D, FL), (FL, D)]
    held = pl.pallas_call(
        functools.partial(kernel, (nx, ny, nz, nc, E)),
        out_shape=[V(s, BF16) for s in shapes],
        in_specs=[anywhere] * 8,
        out_specs=[vmem] * 5,
        scratch_shapes=[
            V((2 * pairs, T), F32), V((pairs, T), jnp.int32), V((pairs, 2, T), jnp.int32),
            V((C2, nz, T, cw), BF16),
            V((nz, 2 * nq, T), BF16),
            V((nz, 2 * nq, T), BF16),
            V((C2, 2, rg, cw), BF16),
            V((C2, 2, 2, rg, cw), BF16),
            V((2, rg, tg), BF16),
            V((2, 3, tg, rg), BF16),
            V((2, rg, 128), F32),
            V((D, 2 * FL), BF16),
            V((FL, D), BF16),
            V((2, R, 2 * FL), F32),
            V((2, R, FL), F32),
            V((2, R, FL), BF16),
            V((2, R, 2 * FL), BF16),
            V((C2, R, cw), BF16),
            V((C2, R, cw), BF16),
            V((C2, 2, rg, cw), BF16),
            V((C2, 2, rg, cw), BF16),
            V((C2, 2, tg, cw), F32),
            V((C2, nz - 1, T, cw), BF16),
            V((C2, nz - 1, T, cw), BF16),
            dma((3,)), dma((3 + C2,)), dma((1,)),
            dma((C2, nz - 1)), dma((C2, nz - 1)),
            dma((1,)), dma((nz - 1,)),
            dma((C2, 2)), dma((C2, 2)),
            dma((C2, 2)), dma((C2, 2)),
            dma((C2,)), dma((C2,)),
            dma((C2, 2)), dma((C2, 2)),
            dma((C2, nz - 1)), dma((C2, nz - 1)),
        ],
        compiler_params=pltpu.CompilerParams(
            collective_id=0, has_side_effects=True, vmem_limit_bytes=38 * 1024 * 1024
        ),
    )(
        *(
            pltpu.with_memory_space_constraint(v, pltpu.HBM)
            for v in (
                tokens, upstream, gate_weights.T, group_choice.T,
                pair_pick.transpose(1, 2, 0), w_gate[0, 0], w_up[0, 0], w_down[0, 0],
            )
        )
    )
    mixed, grad_tokens, gg, gu, gd = pl.pallas_call(
        write_out,
        out_shape=[jax.ShapeDtypeStruct(s, BF16) for s in shapes],
        in_specs=[vmem] * 5,
        out_specs=[anywhere] * 5,
        scratch_shapes=[dma((5,))],
        compiler_params=pltpu.CompilerParams(vmem_limit_bytes=1024 * 1024),
    )(*held)
    return mixed, grad_tokens, gg[None, None], gu[None, None], gd[None, None]


def solution(mesh):
    ny = mesh.shape["group"]
    nz = mesh.shape["inner"] // (2 * XDIM)
    both = ("group", "inner")
    flat, deep, three = P(both, None), P(both, None, None, None), P(both, None, None)
    return jax.shard_map(
        functools.partial(on_device, XDIM, ny, nz, CHUNKS),
        mesh=mesh,
        in_specs=(flat, flat, flat, flat, three, deep, deep, deep),
        out_specs=(flat, flat, deep, deep, deep),
        check_vma=False,
    )
```

```python
import functools

import jax
import jax.numpy as jnp
from jax import lax
from jax.experimental import pallas as pl
from jax.experimental.pallas import tpu as pltpu
from jax.sharding import PartitionSpec as P

MESH = pl.DeviceIdType.MESH
F32 = jnp.float32
BF16 = jnp.bfloat16

XDIM = 4
CHUNKS = 2
DY_AT = 2

NT_DIMS = (((1,), (1,)), ((), ()))
TN_DIMS = (((0,), (0,)), ((), ()))


def dot(a, b, dims=(((1,), (0,)), ((), ()))):
    return lax.dot_general(a, b, dims, preferred_element_type=F32)


def kernel(
    cfg,
    tok_hbm, dy_hbm, gw_hbm, gc_hbm, pp_hbm, wg_hbm, wu_hbm, wd_hbm,
    mixed_ref, gt_ref, gg_ref, gu_ref, gd_ref,
    gw_ref, gc_ref, pp_ref, zx, zg, gsrc, xs, xr, amat, comb, wcol, wgu, wd, acc, dh, hid, dgu,
    osend, orecv, rsend, rrecv, part, tsend, trecv,
    w_sem, i_sem, own_sem, ags_sem, agr_sem, zgs_sem, zgr_sem, xs_sem, xr_sem, fs_sem, fr_sem,
    os_sem, or_sem, rs_sem, rr_sem, ts_sem, tr_sem,
):
    NX, NY, NZ, NC, E = cfg
    NQ = NX * NY
    T, D = tok_hbm.shape
    CW = D // NC
    FL = wd.shape[0]
    NB = NZ
    GB = NB // 2
    S2 = 2 * GB
    RG = NQ * S2
    R = 2 * RG
    TG = GB * T
    HP, HM = NZ // 2, NZ - 1 - NZ // 2
    HA = GB // 2
    pairs = gc_ref.shape[0]
    per_group = E // (pairs * 2)
    lz, ln = NZ.bit_length() - 1, NQ.bit_length() - 1
    lt, lg, l2 = T.bit_length() - 1, GB.bit_length() - 1, S2.bit_length() - 1

    y = lax.axis_index("group")
    inner = lax.axis_index("inner")
    core = lax.rem(inner, 2)
    z = lax.rem(lax.div(inner, 2), NZ)
    x = lax.div(inner, 2 * NZ)
    q_me = y * NX + x

    def place(px, pz, pc):
        return (px * NZ + pz) * 2 + pc

    def z_peer(d):
        return (y, place(x, lax.rem(z + d, NZ), core))

    z_up, z_down = z_peer(1), z_peer(NZ - 1)
    sibling = (y, place(x, z, 1 - core))

    offsets = [(i, j) for i in range(NX) for j in range(NY) if i or j]
    offsets.sort(key=lambda o: (not (o[0] and o[1]), min(o[0], NX - o[0]) + min(o[1], NY - o[1])))
    plane = []
    for i, j in offsets:
        tx, ty = lax.rem(x + i, NX), lax.rem(y + j, NY)
        plane.append((ty * NX + tx, (ty, place(tx, z, core))))

    def rcopy(src, dst, ssem, rsem, dev):
        return pltpu.make_async_remote_copy(
            src_ref=src, dst_ref=dst, send_sem=ssem, recv_sem=rsem, device_id=dev, device_id_type=MESH
        )

    small = [
        pltpu.make_async_copy(a, b, i_sem.at[i])
        for i, (a, b) in enumerate(((gw_hbm, gw_ref), (gc_hbm, gc_ref), (pp_hbm, pp_ref)))
    ]
    rows_in = [
        pltpu.make_async_copy(h.at[:, pl.ds(c * CW, CW)], zx.at[n * NC + c, 0], i_sem.at[3 + n * NC + c])
        for n, h in enumerate((tok_hbm, dy_hbm))
        for c in range(NC)
    ]
    for c in small + rows_in:
        c.start()
    barrier = pltpu.get_barrier_semaphore()
    partners = [z_peer(d) for d in range(1, NZ)] + [dev for _, dev in plane] + [sibling]
    for dev in partners:
        pl.semaphore_signal(barrier, inc=1, device_id=dev, device_id_type=MESH)

    loads = [
        pltpu.make_async_copy(wg_hbm, wgu.at[:, pl.ds(0, FL)], w_sem.at[0]),
        pltpu.make_async_copy(wu_hbm, wgu.at[:, pl.ds(FL, FL)], w_sem.at[1]),
        pltpu.make_async_copy(wd_hbm, wd, w_sem.at[2]),
    ]
    for c in loads:
        c.start()
    for c in small:
        c.wait()

    row = lax.broadcasted_iota(jnp.int32, (E, T), 0)
    table = jnp.zeros((E, T), F32)
    for k in range(2 * pairs):
        ids = gc_ref[k // 2 : k // 2 + 1, :] * per_group + pp_ref[k // 2, k % 2 : k % 2 + 1, :]
        ids = ((ids & (NZ - 1)) << ln) + (ids >> lz)
        table = table + jnp.where(ids == row, gw_ref[k : k + 1, :], 0.0)
    hi = table.astype(BF16)
    gsrc[:, 0:NQ, :] = hi.reshape(NZ, NQ, T)
    gsrc[:, NQ:, :] = (table - hi.astype(F32)).astype(BF16).reshape(NZ, NQ, T)
    for c in rows_in:
        c.wait()
    pl.semaphore_wait(barrier, len(partners))

    def spot(h, down):
        return 0 if h == 0 else (2 * h if down else 2 * h - 1)

    tables = []
    for d in range(1, NZ):
        at = spot(d, False) if d <= HP else spot(NZ - d, True)
        dev = z_peer(d)
        tables.append(rcopy(gsrc.at[lax.rem(z + d, NZ)], zg.at[at], zgs_sem.at[0], zgr_sem.at[at - 1], dev))
    own_table = pltpu.make_async_copy(gsrc.at[z], zg.at[0], own_sem.at[0])

    flying = {}

    def later(key, copies):
        flying[key] = copies

    def sent(key):
        for d in flying.pop(key):
            d.wait_send()

    def ag(c, h):
        out = []
        for down, dev in ((False, z_up), (True, z_down))[: 1 + (h <= HM)]:
            at = spot(h, down)
            out.append(rcopy(zx.at[c, spot(h - 1, down)], zx.at[c, at], ags_sem.at[c, at - 1],
                             agr_sem.at[c, at - 1], dev))
        return out

    def ag_send(c, h, arrived=()):
        copies = ag(c, h)
        for i, d in enumerate(copies):
            if i < len(arrived):
                arrived[i].wait_recv()
            d.start()
        for d in arrived[len(copies) :]:
            d.wait_recv()
        later(("ring", c, h), copies)

    def ring_start(chunks):
        for c in chunks:
            ag_send(c, 1)

    def ag_wait(c, h):
        for d in ag(c, h):
            d.wait_recv()

    def rows_at(q):
        return pl.ds(pl.multiple_of(q * S2, S2), S2)

    def xy_start(key, src, dst, ssem, rsem):
        for tq, dev in plane:
            rcopy(src.at[rows_at(tq)], dst.at[rows_at(q_me)], ssem, rsem, dev).start()
        pltpu.make_async_copy(src.at[rows_at(q_me)], dst.at[rows_at(q_me)], rsem).start()
        away = src.at[pl.ds(0, RG - S2)]
        later(key, [rcopy(away, away, ssem, rsem, sibling)])

    def xy_wait(dst, rsem):
        rcopy(dst, dst, rsem, rsem, sibling).wait_recv()

    def slot_tables(g):
        span = slice(g * GB, (g + 1) * GB)
        whi = zg[span, 0:NQ, :].reshape(GB * NQ, T).astype(F32)
        wlo = zg[span, NQ:, :].reshape(GB * NQ, T).astype(F32)
        routed = whi > 0.0
        i0 = lax.broadcasted_iota(jnp.int32, (T, T), 0)
        i1 = lax.broadcasted_iota(jnp.int32, (T, T), 1)
        earlier = jnp.where(i0 < i1, 1.0, 0.0).astype(BF16)
        rank = dot(jnp.where(routed, 1.0, 0.0).astype(BF16), earlier)
        first = jnp.where(routed & (rank < 0.5), 1.0, 0.0)
        second = jnp.where(routed & (rank > 0.5) & (rank < 1.5), 1.0, 0.0)
        k0 = lax.broadcasted_iota(jnp.int32, (2 * GB * NQ, TG), 0)
        k1 = lax.broadcasted_iota(jnp.int32, (2 * GB * NQ, TG), 1)
        block = ((k0 >> ln) & (GB - 1)) == (k1 >> lt)

        def spread(a, b):
            v = jnp.concatenate([a, b], axis=0)
            return jnp.where(block, jnp.concatenate([v] * GB, axis=1), 0.0).astype(BF16)

        r = lax.broadcasted_iota(jnp.int32, (RG, 2 * GB * NQ), 0)
        k = lax.broadcasted_iota(jnp.int32, (RG, 2 * GB * NQ), 1)
        same = ((r >> l2) == (k & (NQ - 1))) & (((r >> 1) & (GB - 1)) == ((k >> ln) & (GB - 1)))
        sel = jnp.where(same & ((r & 1) == (k >> (ln + lg))), 1.0, 0.0).astype(BF16)
        ones = dot(sel, spread(first, second))
        his = dot(sel, spread(first * whi, second * whi))
        los = dot(sel, spread(first * wlo, second * wlo))
        amat[g] = ones.astype(BF16)
        wcol[g] = jnp.broadcast_to(jnp.sum(his + los, axis=1, keepdims=True), (RG, 128))
        return ones, his, los

    def comb_tables(g, made):
        for n, v in enumerate(made):
            comb[g, n] = jnp.transpose(v).astype(BF16)

    def gather(c, g):
        rows = dot(amat[g], zx[c, g * GB : (g + 1) * GB].reshape(TG, CW))
        if c >= NC:
            rows = rows * wcol[g, :, 0:1]
        xs[c, g] = rows.astype(BF16)
        xy_start(("out", c, g), xs.at[c, g], xr.at[c, 0, g], xs_sem.at[c, g], xr_sem.at[c, g])

    def forward(c, g):
        xy_wait(xr.at[c, 0, g], xr_sem.at[c, g])
        d = rcopy(xr.at[c, 0, g], xr.at[c, 1, g], fs_sem.at[c, g], fr_sem.at[c, g], sibling)
        d.start()
        later(("pass", c, g), [d])

    def forward_wait(c, g):
        rcopy(xr.at[c, 0, g], xr.at[c, 1, g], fs_sem.at[c, g], fr_sem.at[c, g], sibling).wait_recv()

    def rows_of(c, half):
        return xr[c, half].reshape(R, CW)

    def gate_up(c, half):
        v = dot(rows_of(c, half), wgu[c * CW : (c + 1) * CW, :])
        acc[half] = v if c == 0 else acc[half] + v

    def hidden(half):
        v = acc[half]
        g, u = v[:, 0:FL], v[:, FL:]
        hid[half] = (g * jax.nn.sigmoid(g) * u).astype(BF16)

    def d_hidden(c, half):
        cols = slice((c - NC) * CW, (c - NC + 1) * CW)
        v = dot(rows_of(c, half), wd[:, cols], NT_DIMS)
        dh[half] = v if c == NC else dh[half] + v

    def d_gate_up(half):
        v = acc[half]
        g, u = v[:, 0:FL], v[:, FL:]
        s = jax.nn.sigmoid(g)
        d = dh[half]
        dgu[half, :, 0:FL] = (d * u * s * (1.0 + g * (1.0 - s))).astype(BF16)
        dgu[half, :, FL:] = (d * (g * s)).astype(BF16)

    def partial(c, half):
        if c < NC:
            return dot(hid[half], wd[:, c * CW : (c + 1) * CW])
        return dot(dgu[half], wgu[(c - NC) * CW : (c - NC + 1) * CW, :], NT_DIMS)

    def give(c):
        osend[c] = partial(c, 1).astype(BF16)
        d = rcopy(osend.at[c], orecv.at[c], os_sem.at[c], or_sem.at[c], sibling)
        d.start()
        later(("give", c), [d])

    def back_start(c, g):
        xy_start(("back", c, g), rsend.at[c, g], rrecv.at[c, g], rs_sem.at[c, g], rr_sem.at[c, g])

    def send_back(c):
        v = partial(c, 0)
        rcopy(osend.at[c], orecv.at[c], os_sem.at[c], or_sem.at[c], sibling).wait_recv()
        rsend[c] = (v + orecv[c].astype(F32)).astype(BF16).reshape(2, RG, CW)
        back_start(c, 1)

    def combine(c, g):
        xy_wait(rrecv.at[c, g], rr_sem.at[c, g])
        rows = rrecv[c, g]
        if c < NC:
            part[c, g] = dot(comb[g, 1], rows) + dot(comb[g, 2], rows)
        else:
            part[c, g] = dot(comb[g, 0], rows)

    def block_sum(c, at):
        lo = (at % GB) * T
        return part[c, at // GB, lo : lo + T, :]

    def sums(c, n, down):
        at = spot(n, not down)
        dev = z_down if down else z_up
        return rcopy(tsend.at[c, at - 1], trecv.at[c, at - 1], ts_sem.at[c, at - 1], tr_sem.at[c, at - 1], dev)

    def sum_step(c, n):
        copies = []
        for down, hops in ((True, HP), (False, HM)):
            if n > hops:
                continue
            at = spot(n, not down)
            v = block_sum(c, at)
            if n < hops:
                sums(c, n + 1, down).wait_recv()
                v = v + trecv[c, spot(n + 1, not down) - 1].astype(F32)
            tsend[c, at - 1] = v.astype(BF16)
            copies.append(sums(c, n, down))
            copies[-1].start()
        later(("sum", c, n), copies)

    def finish(c):
        v = block_sum(c, 0)
        for down, hops in ((True, HP), (False, HM)):
            if hops:
                sums(c, 1, down).wait_recv()
                v = v + trecv[c, spot(1, not down) - 1].astype(F32)
        ref = mixed_ref if c < NC else gt_ref
        i = c % NC
        ref[:, i * CW : (i + 1) * CW] = v.astype(BF16)

    def grad_gate_up(i):
        rows = xr[i].reshape(2 * R, CW)
        v = dot(rows, dgu[...].reshape(2 * R, 2 * FL), TN_DIMS).astype(BF16)
        gg_ref[i * CW : (i + 1) * CW, :] = v[:, 0:FL]
        gu_ref[i * CW : (i + 1) * CW, :] = v[:, FL:]

    def grad_down(i):
        rows = xr[NC + i].reshape(2 * R, CW)
        gd_ref[:, i * CW : (i + 1) * CW] = dot(hid[...].reshape(2 * R, FL), rows, TN_DIMS).astype(BF16)

    xs_list = list(range(NC))
    dy_list = list(range(NC, 2 * NC))
    for d in tables:
        d.start()
    own_table.start()
    gone = zg.at[pl.ds(0, NB - 1)]
    later("tables", [rcopy(gone, gone, zgs_sem.at[0], zgr_sem.at[0], sibling)])
    ring_start(xs_list)
    own_table.wait()
    for d in tables:
        d.wait_recv()
    made = [slot_tables(0)]

    def ring_step(chunks, h):
        for c in chunks:
            if h < HP:
                ag_send(c, h + 1, ag(c, h))
            else:
                ag_wait(c, h)
            if h == HA:
                gather(c, 0)
            if h == HP:
                gather(c, 1)

    for h in range(1, HP + 1):
        ring_step(xs_list, h)
        if h == DY_AT:
            ring_start(dy_list)
        if h == 1:
            made.append(slot_tables(1))
        if h > DY_AT:
            ring_step(dy_list, h - DY_AT)
    for g in range(2):
        comb_tables(g, made[g])
    first_dy = max(HP - DY_AT, 0) + 1
    for h in range(first_dy, HP):
        ring_step(dy_list, h)
        if h == max(first_dy, 1):
            for c in xs_list:
                forward(c, 0)
    for c in loads:
        c.wait()
    for c in xs_list:
        forward(c, 1)
        gate_up(c, 0)
    ring_step(dy_list, HP)
    for c in xs_list:
        for g in range(2):
            forward_wait(c, g)
        gate_up(c, 1)
    hidden(1)
    for c in xs_list:
        give(c)
    hidden(0)
    for c in xs_list:
        send_back(c)
    for c in dy_list:
        forward(c, 0)
    for c in xs_list:
        back_start(c, 0)
    for c in dy_list:
        forward(c, 1)
        d_hidden(c, 0)
    for c in dy_list:
        for g in range(2):
            forward_wait(c, g)
        d_hidden(c, 1)
    d_gate_up(1)
    for c in dy_list:
        give(c)
    d_gate_up(0)
    for c in dy_list:
        send_back(c)

    def sum_start(chunks):
        for c in chunks:
            combine(c, 1)
            sum_step(c, HP)

    def sum_steps(chunks, n):
        for c in chunks:
            if n == HA:
                combine(c, 0)
            sum_step(c, n)

    sum_start(xs_list)
    for c in dy_list:
        back_start(c, 0)
    grad_down(0)
    for n in range(HP - 1, HA, -1):
        sum_steps(xs_list, n)
    for i in range(1, NC):
        grad_down(i)
    sum_steps(xs_list, HA)
    grad_gate_up(0)
    sum_start(dy_list)
    for n in range(HA - 1, 0, -1):
        sum_steps(xs_list, n)
    for n in range(HP - 1, HA, -1):
        sum_steps(dy_list, n)
    for c in xs_list:
        finish(c)
    for i in range(1, NC):
        grad_gate_up(i)
    for n in range(HA, 0, -1):
        sum_steps(dy_list, n)
    for c in dy_list:
        finish(c)

    for key in list(flying):
        sent(key)


def write_out(*refs):
    n = (len(refs) - 1) // 2
    copies = [pltpu.make_async_copy(refs[i], refs[n + i], refs[-1].at[i]) for i in range(n)]
    for c in copies:
        c.start()
    for c in copies:
        c.wait()


def on_device(nx, ny, nz, nc, tokens, upstream, gate_weights, group_choice, pair_pick, w_gate, w_up, w_down):
    T, D = tokens.shape
    FL = w_gate.shape[-1]
    E = nx * ny * nz
    nq, cw, gb = nx * ny, D // nc, nz // 2
    rg, tg, C2 = nq * 2 * gb, gb * T, 2 * nc
    R = 2 * rg
    pairs = group_choice.shape[1]
    dma = pltpu.SemaphoreType.DMA
    anywhere = pl.BlockSpec(memory_space=pltpu.HBM)
    vmem = pl.BlockSpec(memory_space=pltpu.VMEM)
    V = pltpu.VMEM
    shapes = [(T, D), (T, D), (D, FL), (D, FL), (FL, D)]
    held = pl.pallas_call(
        functools.partial(kernel, (nx, ny, nz, nc, E)),
        out_shape=[V(s, BF16) for s in shapes],
        in_specs=[anywhere] * 8,
        out_specs=[vmem] * 5,
        scratch_shapes=[
            V((2 * pairs, T), F32), V((pairs, T), jnp.int32), V((pairs, 2, T), jnp.int32),
            V((C2, nz, T, cw), BF16),
            V((nz, 2 * nq, T), BF16),
            V((nz, 2 * nq, T), BF16),
            V((C2, 2, rg, cw), BF16),
            V((C2, 2, 2, rg, cw), BF16),
            V((2, rg, tg), BF16),
            V((2, 3, tg, rg), BF16),
            V((2, rg, 128), F32),
            V((D, 2 * FL), BF16),
            V((FL, D), BF16),
            V((2, R, 2 * FL), F32),
            V((2, R, FL), F32),
            V((2, R, FL), BF16),
            V((2, R, 2 * FL), BF16),
            V((C2, R, cw), BF16),
            V((C2, R, cw), BF16),
            V((C2, 2, rg, cw), BF16),
            V((C2, 2, rg, cw), BF16),
            V((C2, 2, tg, cw), F32),
            V((C2, nz - 1, T, cw), BF16),
            V((C2, nz - 1, T, cw), BF16),
            dma((3,)), dma((3 + C2,)), dma((1,)),
            dma((C2, nz - 1)), dma((C2, nz - 1)),
            dma((1,)), dma((nz - 1,)),
            dma((C2, 2)), dma((C2, 2)),
            dma((C2, 2)), dma((C2, 2)),
            dma((C2,)), dma((C2,)),
            dma((C2, 2)), dma((C2, 2)),
            dma((C2, nz - 1)), dma((C2, nz - 1)),
        ],
        compiler_params=pltpu.CompilerParams(
            collective_id=0, has_side_effects=True, vmem_limit_bytes=38 * 1024 * 1024
        ),
    )(
        *(
            pltpu.with_memory_space_constraint(v, pltpu.HBM)
            for v in (
                tokens, upstream, gate_weights.T, group_choice.T,
                pair_pick.transpose(1, 2, 0), w_gate[0, 0], w_up[0, 0], w_down[0, 0],
            )
        )
    )
    mixed, grad_tokens, gg, gu, gd = pl.pallas_call(
        write_out,
        out_shape=[jax.ShapeDtypeStruct(s, BF16) for s in shapes],
        in_specs=[vmem] * 5,
        out_specs=[anywhere] * 5,
        scratch_shapes=[dma((5,))],
        compiler_params=pltpu.CompilerParams(vmem_limit_bytes=1024 * 1024),
    )(*held)
    return mixed, grad_tokens, gg[None, None], gu[None, None], gd[None, None]


def solution(mesh):
    ny = mesh.shape["group"]
    nz = mesh.shape["inner"] // (2 * XDIM)
    both = ("group", "inner")
    flat, deep, three = P(both, None), P(both, None, None, None), P(both, None, None)
    return jax.shard_map(
        functools.partial(on_device, XDIM, ny, nz, CHUNKS),
        mesh=mesh,
        in_specs=(flat, flat, flat, flat, three, deep, deep, deep),
        out_specs=(flat, flat, deep, deep, deep),
        check_vma=False,
    )
```

```python
import functools

import jax
import jax.numpy as jnp
from jax import lax
from jax.experimental import pallas as pl
from jax.experimental.pallas import tpu as pltpu
from jax.sharding import PartitionSpec as P

MESH = pl.DeviceIdType.MESH
F32 = jnp.float32
BF16 = jnp.bfloat16

XDIM = 4
CHUNKS = 4
DY_AT = 2

NT_DIMS = (((1,), (1,)), ((), ()))
TN_DIMS = (((0,), (0,)), ((), ()))


def dot(a, b, dims=(((1,), (0,)), ((), ()))):
    return lax.dot_general(a, b, dims, preferred_element_type=F32)


def kernel(
    cfg,
    tok_hbm, dy_hbm, gw_hbm, gc_hbm, pp_hbm, wg_hbm, wu_hbm, wd_hbm,
    mixed_ref, gt_ref, gg_ref, gu_ref, gd_ref,
    gw_ref, gc_ref, pp_ref, zx, zg, gsrc, xs, xr, amat, comb, wcol, wgu, wd, acc, dh, hid, dgu,
    osend, orecv, rsend, rrecv, part, tsend, trecv,
    w_sem, i_sem, own_sem, ags_sem, agr_sem, zgs_sem, zgr_sem, xs_sem, xr_sem, fs_sem, fr_sem,
    os_sem, or_sem, rs_sem, rr_sem, ts_sem, tr_sem,
):
    NX, NY, NZ, NC, E = cfg
    NQ = NX * NY
    T, D = tok_hbm.shape
    CW = D // NC
    FL = wd.shape[0]
    NB = NZ
    GB = NB // 2
    S2 = 2 * GB
    RG = NQ * S2
    R = 2 * RG
    TG = GB * T
    HP, HM = NZ // 2, NZ - 1 - NZ // 2
    HA = GB // 2
    pairs = gc_ref.shape[0]
    per_group = E // (pairs * 2)
    lz, ln = NZ.bit_length() - 1, NQ.bit_length() - 1
    lt, lg, l2 = T.bit_length() - 1, GB.bit_length() - 1, S2.bit_length() - 1

    y = lax.axis_index("group")
    inner = lax.axis_index("inner")
    core = lax.rem(inner, 2)
    z = lax.rem(lax.div(inner, 2), NZ)
    x = lax.div(inner, 2 * NZ)
    q_me = y * NX + x

    def place(px, pz, pc):
        return (px * NZ + pz) * 2 + pc

    def z_peer(d):
        return (y, place(x, lax.rem(z + d, NZ), core))

    z_up, z_down = z_peer(1), z_peer(NZ - 1)
    sibling = (y, place(x, z, 1 - core))

    offsets = [(i, j) for i in range(NX) for j in range(NY) if i or j]
    offsets.sort(key=lambda o: (not (o[0] and o[1]), min(o[0], NX - o[0]) + min(o[1], NY - o[1])))
    plane = []
    for i, j in offsets:
        tx, ty = lax.rem(x + i, NX), lax.rem(y + j, NY)
        plane.append((ty * NX + tx, (ty, place(tx, z, core))))

    def rcopy(src, dst, ssem, rsem, dev):
        return pltpu.make_async_remote_copy(
            src_ref=src, dst_ref=dst, send_sem=ssem, recv_sem=rsem, device_id=dev, device_id_type=MESH
        )

    small = [
        pltpu.make_async_copy(a, b, i_sem.at[i])
        for i, (a, b) in enumerate(((gw_hbm, gw_ref), (gc_hbm, gc_ref), (pp_hbm, pp_ref)))
    ]
    rows_in = [
        pltpu.make_async_copy(h.at[:, pl.ds(c * CW, CW)], zx.at[n * NC + c, 0], i_sem.at[3 + n * NC + c])
        for n, h in enumerate((tok_hbm, dy_hbm))
        for c in range(NC)
    ]
    for c in small + rows_in:
        c.start()
    barrier = pltpu.get_barrier_semaphore()
    partners = [z_peer(d) for d in range(1, NZ)] + [dev for _, dev in plane] + [sibling]
    for dev in partners:
        pl.semaphore_signal(barrier, inc=1, device_id=dev, device_id_type=MESH)

    loads = [
        pltpu.make_async_copy(wg_hbm, wgu.at[:, pl.ds(0, FL)], w_sem.at[0]),
        pltpu.make_async_copy(wu_hbm, wgu.at[:, pl.ds(FL, FL)], w_sem.at[1]),
        pltpu.make_async_copy(wd_hbm, wd, w_sem.at[2]),
    ]
    for c in loads:
        c.start()
    for c in small:
        c.wait()

    row = lax.broadcasted_iota(jnp.int32, (E, T), 0)
    table = jnp.zeros((E, T), F32)
    for k in range(2 * pairs):
        ids = gc_ref[k // 2 : k // 2 + 1, :] * per_group + pp_ref[k // 2, k % 2 : k % 2 + 1, :]
        ids = ((ids & (NZ - 1)) << ln) + (ids >> lz)
        table = table + jnp.where(ids == row, gw_ref[k : k + 1, :], 0.0)
    hi = table.astype(BF16)
    gsrc[:, 0:NQ, :] = hi.reshape(NZ, NQ, T)
    gsrc[:, NQ:, :] = (table - hi.astype(F32)).astype(BF16).reshape(NZ, NQ, T)
    for c in rows_in:
        c.wait()
    pl.semaphore_wait(barrier, len(partners))

    def spot(h, down):
        return 0 if h == 0 else (2 * h if down else 2 * h - 1)

    tables = []
    for d in range(1, NZ):
        at = spot(d, False) if d <= HP else spot(NZ - d, True)
        dev = z_peer(d)
        tables.append(rcopy(gsrc.at[lax.rem(z + d, NZ)], zg.at[at], zgs_sem.at[0], zgr_sem.at[at - 1], dev))
    own_table = pltpu.make_async_copy(gsrc.at[z], zg.at[0], own_sem.at[0])

    flying = {}

    def later(key, copies):
        flying[key] = copies

    def sent(key):
        for d in flying.pop(key):
            d.wait_send()

    def ag(c, h):
        out = []
        for down, dev in ((False, z_up), (True, z_down))[: 1 + (h <= HM)]:
            at = spot(h, down)
            out.append(rcopy(zx.at[c, spot(h - 1, down)], zx.at[c, at], ags_sem.at[c, at - 1],
                             agr_sem.at[c, at - 1], dev))
        return out

    def ag_send(c, h, arrived=()):
        copies = ag(c, h)
        for i, d in enumerate(copies):
            if i < len(arrived):
                arrived[i].wait_recv()
            d.start()
        for d in arrived[len(copies) :]:
            d.wait_recv()
        later(("ring", c, h), copies)

    def ring_start(chunks):
        for c in chunks:
            ag_send(c, 1)

    def ag_wait(c, h):
        for d in ag(c, h):
            d.wait_recv()

    def rows_at(q):
        return pl.ds(pl.multiple_of(q * S2, S2), S2)

    def xy_start(key, src, dst, ssem, rsem):
        for tq, dev in plane:
            rcopy(src.at[rows_at(tq)], dst.at[rows_at(q_me)], ssem, rsem, dev).start()
        pltpu.make_async_copy(src.at[rows_at(q_me)], dst.at[rows_at(q_me)], rsem).start()
        away = src.at[pl.ds(0, RG - S2)]
        later(key, [rcopy(away, away, ssem, rsem, sibling)])

    def xy_wait(dst, rsem):
        rcopy(dst, dst, rsem, rsem, sibling).wait_recv()

    def slot_tables(g):
        span = slice(g * GB, (g + 1) * GB)
        whi = zg[span, 0:NQ, :].reshape(GB * NQ, T).astype(F32)
        wlo = zg[span, NQ:, :].reshape(GB * NQ, T).astype(F32)
        routed = whi > 0.0
        i0 = lax.broadcasted_iota(jnp.int32, (T, T), 0)
        i1 = lax.broadcasted_iota(jnp.int32, (T, T), 1)
        earlier = jnp.where(i0 < i1, 1.0, 0.0).astype(BF16)
        rank = dot(jnp.where(routed, 1.0, 0.0).astype(BF16), earlier)
        first = jnp.where(routed & (rank < 0.5), 1.0, 0.0)
        second = jnp.where(routed & (rank > 0.5) & (rank < 1.5), 1.0, 0.0)
        k0 = lax.broadcasted_iota(jnp.int32, (2 * GB * NQ, TG), 0)
        k1 = lax.broadcasted_iota(jnp.int32, (2 * GB * NQ, TG), 1)
        block = ((k0 >> ln) & (GB - 1)) == (k1 >> lt)

        def spread(a, b):
            v = jnp.concatenate([a, b], axis=0)
            return jnp.where(block, jnp.concatenate([v] * GB, axis=1), 0.0).astype(BF16)

        r = lax.broadcasted_iota(jnp.int32, (RG, 2 * GB * NQ), 0)
        k = lax.broadcasted_iota(jnp.int32, (RG, 2 * GB * NQ), 1)
        same = ((r >> l2) == (k & (NQ - 1))) & (((r >> 1) & (GB - 1)) == ((k >> ln) & (GB - 1)))
        sel = jnp.where(same & ((r & 1) == (k >> (ln + lg))), 1.0, 0.0).astype(BF16)
        ones = dot(sel, spread(first, second))
        his = dot(sel, spread(first * whi, second * whi))
        los = dot(sel, spread(first * wlo, second * wlo))
        amat[g] = ones.astype(BF16)
        wcol[g] = jnp.broadcast_to(jnp.sum(his + los, axis=1, keepdims=True), (RG, 128))
        return ones, his, los

    def comb_tables(g, made):
        for n, v in enumerate(made):
            comb[g, n] = jnp.transpose(v).astype(BF16)

    def gather(c, g):
        rows = dot(amat[g], zx[c, g * GB : (g + 1) * GB].reshape(TG, CW))
        if c >= NC:
            rows = rows * wcol[g, :, 0:1]
        xs[c, g] = rows.astype(BF16)
        xy_start(("out", c, g), xs.at[c, g], xr.at[c, 0, g], xs_sem.at[c, g], xr_sem.at[c, g])

    def forward(c, g):
        xy_wait(xr.at[c, 0, g], xr_sem.at[c, g])
        d = rcopy(xr.at[c, 0, g], xr.at[c, 1, g], fs_sem.at[c, g], fr_sem.at[c, g], sibling)
        d.start()
        later(("pass", c, g), [d])

    def forward_wait(c, g):
        rcopy(xr.at[c, 0, g], xr.at[c, 1, g], fs_sem.at[c, g], fr_sem.at[c, g], sibling).wait_recv()

    def rows_of(c, half):
        return xr[c, half].reshape(R, CW)

    def gate_up(c, half):
        v = dot(rows_of(c, half), wgu[c * CW : (c + 1) * CW, :])
        acc[half] = v if c == 0 else acc[half] + v

    def hidden(half):
        v = acc[half]
        g, u = v[:, 0:FL], v[:, FL:]
        hid[half] = (g * jax.nn.sigmoid(g) * u).astype(BF16)

    def d_hidden(c, half):
        cols = slice((c - NC) * CW, (c - NC + 1) * CW)
        v = dot(rows_of(c, half), wd[:, cols], NT_DIMS)
        dh[half] = v if c == NC else dh[half] + v

    def d_gate_up(half):
        v = acc[half]
        g, u = v[:, 0:FL], v[:, FL:]
        s = jax.nn.sigmoid(g)
        d = dh[half]
        dgu[half, :, 0:FL] = (d * u * s * (1.0 + g * (1.0 - s))).astype(BF16)
        dgu[half, :, FL:] = (d * (g * s)).astype(BF16)

    def partial(c, half):
        if c < NC:
            return dot(hid[half], wd[:, c * CW : (c + 1) * CW])
        return dot(dgu[half], wgu[(c - NC) * CW : (c - NC + 1) * CW, :], NT_DIMS)

    def give(c):
        osend[c] = partial(c, 1).astype(BF16)
        d = rcopy(osend.at[c], orecv.at[c], os_sem.at[c], or_sem.at[c], sibling)
        d.start()
        later(("give", c), [d])

    def back_start(c, g):
        xy_start(("back", c, g), rsend.at[c, g], rrecv.at[c, g], rs_sem.at[c, g], rr_sem.at[c, g])

    def send_back(c):
        v = partial(c, 0)
        rcopy(osend.at[c], orecv.at[c], os_sem.at[c], or_sem.at[c], sibling).wait_recv()
        rsend[c] = (v + orecv[c].astype(F32)).astype(BF16).reshape(2, RG, CW)
        back_start(c, 1)

    def combine(c, g):
        xy_wait(rrecv.at[c, g], rr_sem.at[c, g])
        rows = rrecv[c, g]
        if c < NC:
            part[c, g] = dot(comb[g, 1], rows) + dot(comb[g, 2], rows)
        else:
            part[c, g] = dot(comb[g, 0], rows)

    def block_sum(c, at):
        lo = (at % GB) * T
        return part[c, at // GB, lo : lo + T, :]

    def sums(c, n, down):
        at = spot(n, not down)
        dev = z_down if down else z_up
        return rcopy(tsend.at[c, at - 1], trecv.at[c, at - 1], ts_sem.at[c, at - 1], tr_sem.at[c, at - 1], dev)

    def sum_step(c, n):
        copies = []
        for down, hops in ((True, HP), (False, HM)):
            if n > hops:
                continue
            at = spot(n, not down)
            v = block_sum(c, at)
            if n < hops:
                sums(c, n + 1, down).wait_recv()
                v = v + trecv[c, spot(n + 1, not down) - 1].astype(F32)
            tsend[c, at - 1] = v.astype(BF16)
            copies.append(sums(c, n, down))
            copies[-1].start()
        later(("sum", c, n), copies)

    def finish(c):
        v = block_sum(c, 0)
        for down, hops in ((True, HP), (False, HM)):
            if hops:
                sums(c, 1, down).wait_recv()
                v = v + trecv[c, spot(1, not down) - 1].astype(F32)
        ref = mixed_ref if c < NC else gt_ref
        i = c % NC
        ref[:, i * CW : (i + 1) * CW] = v.astype(BF16)

    def grad_gate_up(i):
        rows = xr[i].reshape(2 * R, CW)
        v = dot(rows, dgu[...].reshape(2 * R, 2 * FL), TN_DIMS).astype(BF16)
        gg_ref[i * CW : (i + 1) * CW, :] = v[:, 0:FL]
        gu_ref[i * CW : (i + 1) * CW, :] = v[:, FL:]

    def grad_down(i):
        rows = xr[NC + i].reshape(2 * R, CW)
        gd_ref[:, i * CW : (i + 1) * CW] = dot(hid[...].reshape(2 * R, FL), rows, TN_DIMS).astype(BF16)

    xs_list = list(range(NC))
    dy_list = list(range(NC, 2 * NC))
    for d in tables:
        d.start()
    own_table.start()
    gone = zg.at[pl.ds(0, NB - 1)]
    later("tables", [rcopy(gone, gone, zgs_sem.at[0], zgr_sem.at[0], sibling)])
    ring_start(xs_list)
    own_table.wait()
    for d in tables:
        d.wait_recv()
    made = [slot_tables(0)]

    def ring_step(chunks, h):
        for c in chunks:
            if h < HP:
                ag_send(c, h + 1, ag(c, h))
            else:
                ag_wait(c, h)
            if h == HA:
                gather(c, 0)
            if h == HP:
                gather(c, 1)

    for h in range(1, HP + 1):
        ring_step(xs_list, h)
        if h == DY_AT:
            ring_start(dy_list)
        if h == 1:
            made.append(slot_tables(1))
        if h > DY_AT:
            ring_step(dy_list, h - DY_AT)
    for g in range(2):
        comb_tables(g, made[g])
    first_dy = max(HP - DY_AT, 0) + 1
    for h in range(first_dy, HP):
        ring_step(dy_list, h)
        if h == max(first_dy, 1):
            for c in xs_list:
                forward(c, 0)
    for c in loads:
        c.wait()
    for c in xs_list:
        forward(c, 1)
        gate_up(c, 0)
    ring_step(dy_list, HP)
    for c in xs_list:
        for g in range(2):
            forward_wait(c, g)
        gate_up(c, 1)
    hidden(1)
    for c in xs_list:
        give(c)
    hidden(0)
    for c in xs_list:
        send_back(c)
    for c in dy_list:
        forward(c, 0)
    for c in xs_list:
        back_start(c, 0)
    for c in dy_list:
        forward(c, 1)
        d_hidden(c, 0)
    for c in dy_list:
        for g in range(2):
            forward_wait(c, g)
        d_hidden(c, 1)
    d_gate_up(1)
    for c in dy_list:
        give(c)
    d_gate_up(0)
    for c in dy_list:
        send_back(c)

    def sum_start(chunks):
        for c in chunks:
            combine(c, 1)
            sum_step(c, HP)

    def sum_steps(chunks, n):
        for c in chunks:
            if n == HA:
                combine(c, 0)
            sum_step(c, n)

    sum_start(xs_list)
    for c in dy_list:
        back_start(c, 0)
    grad_down(0)
    for n in range(HP - 1, HA, -1):
        sum_steps(xs_list, n)
    for i in range(1, NC):
        grad_down(i)
    sum_steps(xs_list, HA)
    grad_gate_up(0)
    sum_start(dy_list)
    for n in range(HA - 1, 0, -1):
        sum_steps(xs_list, n)
    for n in range(HP - 1, HA, -1):
        sum_steps(dy_list, n)
    for c in xs_list:
        finish(c)
    for i in range(1, NC):
        grad_gate_up(i)
    for n in range(HA, 0, -1):
        sum_steps(dy_list, n)
    for c in dy_list:
        finish(c)

    for key in list(flying):
        sent(key)


def write_out(*refs):
    n = (len(refs) - 1) // 2
    copies = [pltpu.make_async_copy(refs[i], refs[n + i], refs[-1].at[i]) for i in range(n)]
    for c in copies:
        c.start()
    for c in copies:
        c.wait()


def on_device(nx, ny, nz, nc, tokens, upstream, gate_weights, group_choice, pair_pick, w_gate, w_up, w_down):
    T, D = tokens.shape
    FL = w_gate.shape[-1]
    E = nx * ny * nz
    nq, cw, gb = nx * ny, D // nc, nz // 2
    rg, tg, C2 = nq * 2 * gb, gb * T, 2 * nc
    R = 2 * rg
    pairs = group_choice.shape[1]
    dma = pltpu.SemaphoreType.DMA
    anywhere = pl.BlockSpec(memory_space=pltpu.HBM)
    vmem = pl.BlockSpec(memory_space=pltpu.VMEM)
    V = pltpu.VMEM
    shapes = [(T, D), (T, D), (D, FL), (D, FL), (FL, D)]
    held = pl.pallas_call(
        functools.partial(kernel, (nx, ny, nz, nc, E)),
        out_shape=[V(s, BF16) for s in shapes],
        in_specs=[anywhere] * 8,
        out_specs=[vmem] * 5,
        scratch_shapes=[
            V((2 * pairs, T), F32), V((pairs, T), jnp.int32), V((pairs, 2, T), jnp.int32),
            V((C2, nz, T, cw), BF16),
            V((nz, 2 * nq, T), BF16),
            V((nz, 2 * nq, T), BF16),
            V((C2, 2, rg, cw), BF16),
            V((C2, 2, 2, rg, cw), BF16),
            V((2, rg, tg), BF16),
            V((2, 3, tg, rg), BF16),
            V((2, rg, 128), F32),
            V((D, 2 * FL), BF16),
            V((FL, D), BF16),
            V((2, R, 2 * FL), F32),
            V((2, R, FL), F32),
            V((2, R, FL), BF16),
            V((2, R, 2 * FL), BF16),
            V((C2, R, cw), BF16),
            V((C2, R, cw), BF16),
            V((C2, 2, rg, cw), BF16),
            V((C2, 2, rg, cw), BF16),
            V((C2, 2, tg, cw), F32),
            V((C2, nz - 1, T, cw), BF16),
            V((C2, nz - 1, T, cw), BF16),
            dma((3,)), dma((3 + C2,)), dma((1,)),
            dma((C2, nz - 1)), dma((C2, nz - 1)),
            dma((1,)), dma((nz - 1,)),
            dma((C2, 2)), dma((C2, 2)),
            dma((C2, 2)), dma((C2, 2)),
            dma((C2,)), dma((C2,)),
            dma((C2, 2)), dma((C2, 2)),
            dma((C2, nz - 1)), dma((C2, nz - 1)),
        ],
        compiler_params=pltpu.CompilerParams(
            collective_id=0, has_side_effects=True, vmem_limit_bytes=38 * 1024 * 1024
        ),
    )(
        *(
            pltpu.with_memory_space_constraint(v, pltpu.HBM)
            for v in (
                tokens, upstream, gate_weights.T, group_choice.T,
                pair_pick.transpose(1, 2, 0), w_gate[0, 0], w_up[0, 0], w_down[0, 0],
            )
        )
    )
    mixed, grad_tokens, gg, gu, gd = pl.pallas_call(
        write_out,
        out_shape=[jax.ShapeDtypeStruct(s, BF16) for s in shapes],
        in_specs=[vmem] * 5,
        out_specs=[anywhere] * 5,
        scratch_shapes=[dma((5,))],
        compiler_params=pltpu.CompilerParams(vmem_limit_bytes=1024 * 1024),
    )(*held)
    return mixed, grad_tokens, gg[None, None], gu[None, None], gd[None, None]


def solution(mesh):
    ny = mesh.shape["group"]
    nz = mesh.shape["inner"] // (2 * XDIM)
    both = ("group", "inner")
    flat, deep, three = P(both, None), P(both, None, None, None), P(both, None, None)
    return jax.shard_map(
        functools.partial(on_device, XDIM, ny, nz, CHUNKS),
        mesh=mesh,
        in_specs=(flat, flat, flat, flat, three, deep, deep, deep),
        out_specs=(flat, flat, deep, deep, deep),
        check_vma=False,
    )
```
